32 devices in a mesh: gx: 4 (over y, core), gy: 4 (over z), gz: 2 (over x).
Axes of the slice: x: 2, y: 2, z: 4, core: 2. Of those that a mesh axis runs over, the one named last changes fastest.
Arguments:
- right_sides: float32 [6, 128, 128, 256], P(None, 'gx', 'gy', 'gz'), may hold values from -6 to 6
- permeability: float32 [128, 128, 256], P('gx', 'gy', 'gz'), may hold values from 0.1 to 10
Outputs:
- basis_q: float32 [24, 128, 128, 256], P(None, 'gx', 'gy', 'gz')
- factor_r: float32 [24, 24], replicated
The draws below stay inside these ranges and needn't reach their ends.
All inputs are finite; a program needn't handle non-finite values.
Results may differ from the reference program's by a relative error of at most 0.00012.
Values sent between devices are 32-bit elements; how exact they have to be, the bound alone decides.
No kernel may reach another device: no remote copies, remote signals or barrier semaphores. Data moves between devices by JAX's collectives and lax.ppermute only.
A program may use at most 128 MiB of HBM per device.

```python
import math
import jax
import jax.numpy as jnp
from jax import lax

NRHS = 6
SSTEP = 3
NCOL = 24
NX = 128
NY = 128
NZ = 256
CELLS = 4194304


def steps_of(stream_key, dims, pieces, smallest, high):
    factor_of = 1.0
    for axis_at, parts in pieces:
        draws = jax.random.uniform(jax.random.fold_in(jax.random.fold_in(stream_key, 6), axis_at), (parts,), jnp.float32, smallest / len(pieces), high / len(pieces))
        factor_of = factor_of * jnp.repeat(jnp.exp(draws), dims[axis_at] // parts).reshape((-1,) + (1,) * (len(dims) - 1 - axis_at))
    return factor_of


def centred(key, dims, deviation, bound, cuts=(), dtype=jnp.bfloat16):
    entries = deviation * jax.random.normal(key, dims, jnp.float32)
    if cuts:
        entries = entries * steps_of(key, dims, cuts, -0.22, 0.18)
    return jnp.clip(entries, -bound, bound).astype(dtype)


def setup_inputs(seed: int = 0) -> dict:
    streams_of = jax.random.split(jax.random.key(seed), 3)
    right_sides = centred(streams_of[0], (NRHS, NX, NY, NZ), 1.0, 6.0, ((1, 4), (2, 4), (3, 2)), jnp.float32)
    permeability = jnp.clip(jnp.exp(math.log(10.0) - 4.6051702 * jax.random.uniform(streams_of[1], (NX, NY, NZ), jnp.float32) ** steps_of(streams_of[1], (NX, NY, NZ), ((0, 4), (1, 4), (2, 2)), -0.2, 0.2)), 0.1, 10.0)
    return dict(right_sides=right_sides, permeability=permeability)


def face_weights(kappa_pad):
    center = kappa_pad[1:-1, 1:-1, 1:-1]
    others = [kappa_pad[2:, 1:-1, 1:-1], kappa_pad[:-2, 1:-1, 1:-1], kappa_pad[1:-1, 2:, 1:-1], kappa_pad[1:-1, :-2, 1:-1], kappa_pad[1:-1, 1:-1, 2:], kappa_pad[1:-1, 1:-1, :-2]]
    face_list = [2.0 * center * neighbour / (center + neighbour) for neighbour in others]
    diagonal = face_list[0]
    for weight in face_list[1:]:
        diagonal = diagonal + weight
    return (face_list, diagonal)

def stencil(field_pad, face_list, diagonal):
    slices = [field_pad[:, 2:, 1:-1, 1:-1], field_pad[:, :-2, 1:-1, 1:-1], field_pad[:, 1:-1, 2:, 1:-1], field_pad[:, 1:-1, :-2, 1:-1], field_pad[:, 1:-1, 1:-1, 2:], field_pad[:, 1:-1, 1:-1, :-2]]
    accum = face_list[0] * slices[0]
    for weight, piece in zip(face_list[1:], slices[1:]):
        accum = accum + weight * piece
    return 2.5 * accum / diagonal

def reference(right_sides, permeability):
    kappa_pad = jnp.pad(permeability, 1)
    face_list, diagonal = face_weights(kappa_pad)
    powers = [right_sides]
    field = right_sides
    for power_index in range(SSTEP):
        padded = jnp.pad(field, ((0, 0), (1, 1), (1, 1), (1, 1)))
        field = stencil(padded, face_list, diagonal)
        powers.append(field)
    basis = jnp.concatenate(powers, 0)
    flat = basis.reshape(NCOL, -1)
    gram = jnp.dot(flat, flat.T, precision=lax.Precision.HIGHEST)
    factor_r = jnp.linalg.cholesky(gram / CELLS).T
    solved = lax.linalg.triangular_solve(factor_r, flat, left_side=True, lower=False, transpose_a=True)
    return (solved.reshape(basis.shape), factor_r)
```

```python
import functools

import jax
import jax.numpy as jnp
from jax import lax
from jax.experimental import pallas as pl
from jax.experimental.pallas import tpu as pltpu
from jax.sharding import PartitionSpec as P

F32 = jnp.float32
BF16 = jnp.bfloat16
DEPTH = 3
LANES = 128
TOP = 8
MIB = 1 << 20


def even_on(axis):
    return lax.rem(lax.axis_index(axis), 2) == 0


def lane_index(rows=8):
    return lax.broadcasted_iota(jnp.int32, (rows, LANES), 1)


def take_lanes(tile, lanes):
    return jnp.take_along_axis(tile, lanes, axis=1)


def pair_exchange(first, second, axis):
    count = lax.axis_size(axis)
    firsts = [(i, i + 1) for i in range(0, count - 1, 2)]
    seconds = [(i, i + 1) for i in range(1, count - 1, 2)]
    got_first = lax.ppermute(first, axis, [p for a, b in firsts for p in ((a, b), (b, a))])
    if not seconds:
        return (got_first,)
    got_second = lax.ppermute(second, axis, [p for a, b in seconds for p in ((a, b), (b, a))])
    return (got_first, got_second)


def pack_faces(rs_ref, k_ref, pad_ref, xa_ref, xb_ref, ya_ref, yb_ref, sems):
    fields = rs_ref.shape[0]
    nx, ny = k_ref.shape[0], k_ref.shape[1]
    copies = [
        pltpu.make_async_copy(
            rs_ref.at[f], pad_ref.at[f, pl.ds(DEPTH, nx), pl.ds(TOP, ny)], sems.at[f]
        )
        for f in range(fields)
    ]
    copies.append(
        pltpu.make_async_copy(
            k_ref, pad_ref.at[fields, pl.ds(DEPTH, nx), pl.ds(TOP, ny)], sems.at[fields]
        )
    )
    for copy in copies:
        copy.start()
    ex, ey = even_on("gx"), even_on("gy")
    start_a = jnp.where(ex, nx, DEPTH)
    start_b = jnp.where(ex, DEPTH, nx)
    for f in range(fields + 1):
        copies[f].wait()
        for i in range(DEPTH):
            xa_ref[f, i] = pad_ref[f, start_a + i, TOP : TOP + ny, :]
            xb_ref[f, i] = pad_ref[f, start_b + i, TOP : TOP + ny, :]
        for x in range(nx):
            low = pad_ref[f, x + DEPTH, TOP : TOP + DEPTH, :]
            high = pad_ref[f, x + DEPTH, TOP + ny - DEPTH : TOP + ny, :]
            row = DEPTH * (f * nx + x)
            ya_ref[row : row + DEPTH, :] = jnp.where(ey, high, low)
            yb_ref[row : row + DEPTH, :] = jnp.where(ey, low, high)


def pack_edges(xa_ref, xb_ref, ea_ref, eb_ref):
    fields, _, ny, _ = xa_ref.shape
    ex, ey = even_on("gx"), even_on("gy")
    for f in range(fields):
        for side in range(2):
            for i in range(DEPTH):
                a, b = xa_ref, xb_ref
                if side == 0:
                    low = jnp.where(ex, b[f, i, :DEPTH, :], a[f, i, :DEPTH, :])
                    high = jnp.where(ex, b[f, i, ny - DEPTH :, :], a[f, i, ny - DEPTH :, :])
                else:
                    low = jnp.where(ex, a[f, i, :DEPTH, :], b[f, i, :DEPTH, :])
                    high = jnp.where(ex, a[f, i, ny - DEPTH :, :], b[f, i, ny - DEPTH :, :])
                row = DEPTH * ((f * 2 + side) * DEPTH + i)
                ea_ref[row : row + DEPTH, :] = jnp.where(ey, high, low)
                eb_ref[row : row + DEPTH, :] = jnp.where(ey, low, high)


def assemble(nx, ny, two_z, pad_in, xa, xb, ya, yb, ea, eb, *outs):
    del pad_in
    if two_z:
        pad, own, za, zb = outs
    else:
        pad, own, za = outs
        zb = None
    slabs = pad.shape[0]
    ex, ey, ez = even_on("gx"), even_on("gy"), even_on("gz")
    bottom = TOP + ny
    wide = nx + 2 * DEPTH
    half = wide // 2
    tiles = (ny + 2 * DEPTH + 7) // 8
    for f in range(slabs):
        for i in range(DEPTH):
            a, b = xa[f, i], xb[f, i]
            pad[f, i, TOP:bottom, :] = jnp.where(ex, b, a)
            pad[f, nx + DEPTH + i, TOP:bottom, :] = jnp.where(ex, a, b)
        for x in range(nx):
            row = DEPTH * (f * nx + x)
            a, b = ya[row : row + DEPTH, :], yb[row : row + DEPTH, :]
            pad[f, x + DEPTH, TOP - DEPTH : TOP, :] = jnp.where(ey, b, a)
            pad[f, x + DEPTH, bottom : bottom + DEPTH, :] = jnp.where(ey, a, b)
        for side in range(2):
            for i in range(DEPTH):
                row = DEPTH * ((f * 2 + side) * DEPTH + i)
                plane = i if side == 0 else nx + DEPTH + i
                a, b = ea[row : row + DEPTH, :], eb[row : row + DEPTH, :]
                pad[f, plane, TOP - DEPTH : TOP, :] = jnp.where(ey, b, a)
                pad[f, plane, bottom : bottom + DEPTH, :] = jnp.where(ey, a, b)

    lane = lane_index()
    place = lane // 2
    is_left = lane % 2 == 1
    column = lane % wide
    step = jnp.minimum(lane // wide, DEPTH - 1)

    def from_halves(first, second, at, zs):
        in_first = at < half
        index = 6 * jnp.where(in_first, at, jnp.minimum(at - half, half - 1)) + zs
        return jnp.where(in_first, take_lanes(first, index), take_lanes(second, index))

    @pl.loop(0, slabs)
    def _(f):
        for t in range(tiles):
            rows = slice(TOP - DEPTH + 8 * t, TOP - DEPTH + 8 * t + 8)
            packed = []
            for part in range(2):
                acc = jnp.zeros((8, LANES), F32)
                for m in range(half):
                    tile = pad[f, part * half + m, rows, :]
                    moved = pltpu.roll(tile, 6 * m + 3, 1)
                    acc = jnp.where(lane // 6 == m, moved, acc)
                packed.append(acc)
            first, second = packed
            out = slice(8 * t, 8 * t + 8)
            for j in range(2):
                own[f, j, out, :] = from_halves(
                    first, second, place, jnp.where(is_left, 3 + j, 2 - j)
                )
            to_left, to_right = 3 + step, 2 - step
            za[f, out, :] = from_halves(first, second, column, jnp.where(ez, to_right, to_left))
            if two_z:
                zb[f, out, :] = from_halves(
                    first, second, column, jnp.where(ez, to_left, to_right)
                )


def face(center, other):
    total = center + other
    return 2.0 * center * other / jnp.where(total > 0, total, 1.0)


def scaled_faces(center, others):
    faces = [face(center, other) for other in others]
    diagonal = faces[0]
    for weight in faces[1:]:
        diagonal = diagonal + weight
    scale = 2.5 / jnp.where(diagonal > 0, diagonal, 1.0)
    return [weight * scale for weight in faces]


def weighted(weights, values):
    accum = weights[0] * values[0]
    for weight, value in zip(weights[1:], values[1:]):
        accum = accum + weight * value
    return accum


def powers(nx, ny, two_z, pad, own, za, *rest):
    if two_z:
        zb, rest = rest[0], rest[1:]
    else:
        zb = None
    high_ref, low_ref, gram_ref, coef, v1, v2, strip, scoef, s1, s2, acc, square = rest
    fields = pad.shape[0] - 1
    wide = nx + 2 * DEPTH
    ez = even_on("gz")
    lane = lane_index()
    place = lane // 2
    is_left = lane % 2 == 1
    tiles = (ny + 2 * DEPTH + 7) // 8

    @pl.loop(0, fields + 1)
    def _(f):
        for t in range(tiles):
            rows = slice(8 * t, 8 * t + 8)
            got_a = za[f, rows, :]
            if two_z:
                got_b = zb[f, rows, :]
                left = jnp.where(ez, got_b, got_a)
                right = jnp.where(ez, got_a, got_b)
            for q in range(DEPTH):
                index = jnp.minimum(wide * (DEPTH - 1 - q) + place, LANES - 1)
                if two_z:
                    tile = jnp.where(is_left, take_lanes(left, index), take_lanes(right, index))
                else:
                    keep = is_left != ez
                    tile = jnp.where(keep, take_lanes(got_a, index), 0.0)
                strip[f, q, rows, :] = tile
            for j in range(2):
                strip[f, DEPTH + j, rows, :] = own[f, j, rows, :]

    def strip_neighbours(ref, f, q, base, row):
        rows = slice(row, row + 8)
        tile = ref[f, q - base, rows, :]
        return tile, [
            pltpu.roll(tile, LANES - 2, 1),
            pltpu.roll(tile, 2, 1),
            ref[f, q - base, row + 1 : row + 9, :],
            ref[f, q - base, row - 1 : row + 7, :],
            ref[f, q + 1 - base, rows, :],
            ref[f, q - 1 - base, rows, :],
        ]

    for q in range(1, 4):
        for t in range(tiles):
            row = 1 + 8 * t
            center, others = strip_neighbours(strip, fields, q, 0, row)
            for n, weight in enumerate(scaled_faces(center, others)):
                scoef[n, q - 1, row : row + 8, :] = weight

    @pl.loop(0, fields)
    def _(f):
        for q in range(1, 4):
            for t in range(tiles):
                row = 1 + 8 * t
                weights = [scoef[n, q - 1, row : row + 8, :] for n in range(6)]
                _, values = strip_neighbours(strip, f, q, 0, row)
                s1[f, q - 1, row : row + 8, :] = weighted(weights, values)
        for t in range(tiles):
            row = 2 + 8 * t
            weights = [scoef[n, 1, row : row + 8, :] for n in range(6)]
            _, values = strip_neighbours(s1, f, 2, 1, row)
            s2[f, row : row + 8, :] = weighted(weights, values)

    def z_pair(tile, edge, plane):
        moved = pltpu.roll(edge, LANES - 1 - 2 * plane, 1)
        return [
            jnp.where(lane == LANES - 1, moved, pltpu.roll(tile, LANES - 1, 1)),
            jnp.where(lane == 0, moved, pltpu.roll(tile, 1, 1)),
        ]

    @pl.loop(0, nx + 4)
    def _(i):
        plane = i + 1
        for t in range(tiles):
            y = 8 * t - 2
            r = TOP + y
            tile = pad[fields, plane, r : r + 8, :]
            others = [
                pad[fields, plane + 1, r : r + 8, :],
                pad[fields, plane - 1, r : r + 8, :],
                pad[fields, plane, r + 1 : r + 9, :],
                pad[fields, plane, r - 1 : r + 7, :],
            ] + z_pair(tile, strip[fields, 2, y + 3 : y + 11, :], plane)
            for n, weight in enumerate(scaled_faces(tile, others)):
                coef[n, i, 8 * t : 8 * t + 8, :] = weight

    def advance(source, source_x, edge, f, plane, y, weights):
        r = TOP + y
        s = plane - source_x
        tile = source[f, s, r : r + 8, :]
        values = [
            source[f, s + 1, r : r + 8, :],
            source[f, s - 1, r : r + 8, :],
            source[f, s, r + 1 : r + 9, :],
            source[f, s, r - 1 : r + 7, :],
        ] + z_pair(tile, edge, plane)
        return weighted(weights, values)

    def weights_at(plane, y):
        return [coef[n, plane - 1, y + 2 : y + 10, :] for n in range(6)]

    @pl.loop(1, nx + 5)
    def _(plane):
        for t in range(tiles):
            y = 8 * t - 2
            weights = weights_at(plane, y)
            for f in range(fields):
                edge = strip[f, 2, y + 3 : y + 11, :]
                v1[f, plane - 1, TOP + y : TOP + y + 8, :] = advance(
                    pad, 0, edge, f, plane, y, weights
                )

    @pl.loop(2, nx + 4)
    def _(plane):
        for t in range(tiles):
            y = 8 * t - 1
            weights = weights_at(plane, y)
            for f in range(fields):
                edge = s1[f, 1, y + 3 : y + 11, :]
                v2[f, plane - 2, TOP + y : TOP + y + 8, :] = advance(
                    v1, 1, edge, f, plane, y, weights
                )

    blocks = ny // 8

    def last_power(plane):
        for t in range(blocks):
            y = 8 * t
            rows = slice(TOP + y, TOP + y + 8)
            weights = weights_at(plane, y)
            columns = [pad[f, plane, rows, :] for f in range(fields)]
            columns += [v1[f, plane - 1, rows, :] for f in range(fields)]
            columns += [v2[f, plane - 2, rows, :] for f in range(fields)]
            for f in range(fields):
                edge = s2[f, y + 3 : y + 11, :]
                columns.append(advance(v2, 2, edge, f, plane, y, weights))
            block = (plane - DEPTH) * blocks + t
            for g in range(len(columns) // 2):
                pair = jnp.concatenate(columns[2 * g : 2 * g + 2], 0)
                high = pair.astype(BF16)
                high_ref[block, 16 * g : 16 * g + 16, :] = high
                low_ref[block, 16 * g : 16 * g + 16, :] = (pair - high.astype(F32)).astype(BF16)

    def products(plane):
        base = (plane - DEPTH) * blocks
        high = jnp.concatenate([high_ref[base + t] for t in range(blocks)], 1)
        low = jnp.concatenate([low_ref[base + t] for t in range(blocks)], 1)
        both = jnp.concatenate([high, low], 0)
        acc[...] += lax.dot_general(
            both, high, (((1,), (1,)), ((), ())), preferred_element_type=F32
        )

    acc[...] = jnp.zeros_like(acc)
    last_power(DEPTH)

    @pl.loop(DEPTH + 1, nx + DEPTH)
    def _(plane):
        last_power(plane)
        products(plane - 1)

    products(nx + DEPTH - 1)

    rows = acc.shape[1]
    sums = acc[...]
    same = lax.broadcasted_iota(jnp.int32, sums.shape, 0) % 8 == (
        lax.broadcasted_iota(jnp.int32, sums.shape, 1) % 8
    )
    sums = jnp.where(same, sums, 0.0).reshape(2 * rows // 8, 8, rows).sum(1)
    pick = lax.broadcasted_iota(jnp.int32, (rows, LANES), 0) // 8 == (
        lax.broadcasted_iota(jnp.int32, (rows, LANES), 1)
    )
    small = jnp.dot(sums, pick.astype(F32), precision=lax.Precision.HIGHEST)
    order = rows // 8
    square[...] = jnp.zeros_like(square)
    square[0:order, :] = small[order : 2 * order, :]
    cross = small[order : 2 * order, :]
    gram_ref[...] = small[0:order, :] + cross + square[...].T[0:order, :]


def factor_and_solve(cells, order, ny, gram_a, gram_b, high_ref, low_ref, out_ref, factor_ref, w_wide, w_low):
    blocks = ny // 8
    rows = 8 * order

    @pl.when(pl.program_id(0) == 0)
    def _():
        row = lax.broadcasted_iota(jnp.int32, (order, LANES), 0)
        lane = lax.broadcasted_iota(jnp.int32, (order, LANES), 1)
        work = (gram_a[...] + gram_b[...]) / cells
        work = jnp.where(lane < order, work, jnp.where(lane == row + 64, 1.0, 0.0))
        for j in range(order):
            pivot = work[j : j + 1, :]
            factor = work[:, j : j + 1] / work[j : j + 1, j : j + 1]
            work = work - jnp.where(row > j, factor * pivot, 0.0)
        pivots = jnp.sum(jnp.where(lane == row, work, 0.0), 1, keepdims=True)
        work = work / jnp.sqrt(pivots)
        factor_ref[...] = jnp.where(lane >= row, work, 0.0)[:, :order]
        inverse = pltpu.roll(work, 64, 1)
        inverse = jnp.where(lane <= row, inverse, 0.0)
        high = inverse.astype(BF16)
        low = (inverse - high.astype(F32)).astype(BF16)
        spread = (
            lax.broadcasted_iota(jnp.int32, (rows, order), 0) // 8
            == lax.broadcasted_iota(jnp.int32, (rows, order), 1)
        ).astype(BF16)
        across = (
            lax.broadcasted_iota(jnp.int32, (LANES, rows), 1) // 8
            == lax.broadcasted_iota(jnp.int32, (LANES, rows), 0)
        ).astype(BF16)
        same = lax.broadcasted_iota(jnp.int32, (rows, rows), 0) % 8 == (
            lax.broadcasted_iota(jnp.int32, (rows, rows), 1) % 8
        )

        def kron(small):
            tall = jnp.dot(spread, small, preferred_element_type=F32).astype(BF16)
            full = jnp.dot(tall, across, preferred_element_type=F32)
            return jnp.where(same, full, 0.0).astype(BF16)

        w_high = kron(high)
        w_wide[:, :rows] = w_high
        w_wide[:, rows:] = w_high
        w_low[...] = kron(low)

    base = pl.program_id(0) * blocks
    high = jnp.concatenate([high_ref[base + t] for t in range(blocks)], 1)
    low = jnp.concatenate([low_ref[base + t] for t in range(blocks)], 1)
    both = jnp.concatenate([high, low], 0)
    result = jnp.dot(w_wide[...], both, preferred_element_type=F32)
    result = result + jnp.dot(w_low[...], high, preferred_element_type=F32)
    for t in range(blocks):
        for b in range(order):
            out_ref[b, 0, 8 * t : 8 * t + 8, :] = result[
                8 * b : 8 * b + 8, LANES * t : LANES * t + LANES
            ]


VM = functools.partial(pl.BlockSpec, memory_space=pltpu.VMEM)


def params(limit):
    return pltpu.CompilerParams(vmem_limit_bytes=limit * MIB)


def on_device(right_sides, permeability):
    fields, nx, ny, nz = right_sides.shape
    slabs = fields + 1
    order = fields * (DEPTH + 1)
    rows = 8 * order
    tall = ny + 16
    wide = nx + 2 * DEPTH
    strip_rows = 8 * ((ny + 2 * DEPTH + 7) // 8)
    two_z = lax.axis_size("gz") > 2
    devices = lax.axis_size("gx") * lax.axis_size("gy") * lax.axis_size("gz")
    cells = float(nx * ny * nz * devices)

    pad_type = pltpu.VMEM((slabs, wide, tall, LANES), F32)
    x_type = pltpu.VMEM((slabs, DEPTH, ny, LANES), F32)
    y_type = pltpu.VMEM((slabs * nx * DEPTH, LANES), F32)
    e_rows = 8 * ((slabs * 2 * DEPTH * DEPTH + 7) // 8)
    e_type = pltpu.VMEM((e_rows, LANES), F32)
    pad, xa, xb, ya, yb = pl.pallas_call(
        pack_faces,
        out_shape=(pad_type, x_type, x_type, y_type, y_type),
        in_specs=[pl.BlockSpec(memory_space=pl.ANY)] * 2,
        out_specs=(VM(),) * 5,
        scratch_shapes=[pltpu.SemaphoreType.DMA((slabs,))],
        compiler_params=params(8),
        name="pack_faces",
    )(right_sides, permeability)
    got_xa, got_xb = pair_exchange(xa, xb, "gx")
    got_ya, got_yb = pair_exchange(ya, yb, "gy")
    ea, eb = pl.pallas_call(
        pack_edges,
        out_shape=(e_type, e_type),
        in_specs=[VM()] * 2,
        out_specs=(VM(),) * 2,
        compiler_params=params(8),
        name="pack_edges",
    )(got_xa, got_xb)
    got_ea, got_eb = pair_exchange(ea, eb, "gy")

    own_type = pltpu.VMEM((slabs, 2, strip_rows, LANES), F32)
    z_type = pltpu.VMEM((slabs, strip_rows, LANES), F32)
    z_count = 2 if two_z else 1
    outs = pl.pallas_call(
        functools.partial(assemble, nx, ny, two_z),
        out_shape=(pad_type, own_type) + (z_type,) * z_count,
        in_specs=[VM()] * 7,
        out_specs=(VM(),) * (2 + z_count),
        input_output_aliases={0: 0},
        compiler_params=params(8),
        name="assemble",
    )(pad, got_xa, got_xb, got_ya, got_yb, got_ea, got_eb)
    pad, own = outs[:2]
    got_z = pair_exchange(outs[2], outs[-1], "gz")

    blocks = nx * ny // 8
    split_type = pltpu.VMEM((blocks, rows, LANES), BF16)
    high, low, gram = pl.pallas_call(
        functools.partial(powers, nx, ny, two_z),
        out_shape=(split_type, split_type, pltpu.VMEM((order, LANES), F32)),
        in_specs=[VM()] * (2 + len(got_z)),
        out_specs=(VM(),) * 3,
        scratch_shapes=[
            pltpu.VMEM((6, nx + 4, tall, LANES), F32),
            pltpu.VMEM((fields, nx + 4, tall, LANES), F32),
            pltpu.VMEM((fields, nx + 2, tall, LANES), F32),
            pltpu.VMEM((slabs, 5, tall, LANES), F32),
            pltpu.VMEM((6, 3, tall, LANES), F32),
            pltpu.VMEM((fields, 3, tall, LANES), F32),
            pltpu.VMEM((fields, tall, LANES), F32),
            pltpu.VMEM((2 * rows, rows), F32),
            pltpu.VMEM((LANES, LANES), F32),
        ],
        compiler_params=params(26),
        name="powers",
    )(pad, own, *got_z)

    stages = []
    for axis in ("gz", "gx", "gy"):
        count, stride = lax.axis_size(axis), 1
        while stride < count:
            stages.append((axis, [(i, i ^ stride) for i in range(count)]))
            stride *= 2
    for axis, pairs in stages[:-1]:
        gram = gram + lax.ppermute(gram, axis, pairs)
    other = lax.ppermute(gram, *stages[-1])

    basis_q, factor_r = pl.pallas_call(
        functools.partial(factor_and_solve, cells, order, ny),
        grid=(nx,),
        out_shape=(
            jax.ShapeDtypeStruct((order, nx, ny, nz), F32),
            jax.ShapeDtypeStruct((order, order), F32),
        ),
        in_specs=[VM()] * 4,
        out_specs=(
            pl.BlockSpec((order, 1, ny, nz), lambda i: (0, i, 0, 0)),
            pl.BlockSpec((order, order), lambda i: (0, 0)),
        ),
        scratch_shapes=[pltpu.VMEM((rows, 2 * rows), BF16), pltpu.VMEM((rows, rows), BF16)],
        compiler_params=params(16),
        name="factor_and_solve",
    )(gram, other, high, low)
    return (basis_q, factor_r)


def solution(mesh):
    placed = (P(None, "gx", "gy", "gz"), P("gx", "gy", "gz"))
    return jax.shard_map(
        on_device,
        mesh=mesh,
        in_specs=placed,
        out_specs=(P(None, "gx", "gy", "gz"), P()),
        check_vma=False,
    )
```

```python
import functools

import jax
import jax.numpy as jnp
from jax import lax
from jax.experimental import pallas as pl
from jax.experimental.pallas import tpu as pltpu
from jax.sharding import PartitionSpec as P

F32 = jnp.float32
BF16 = jnp.bfloat16
DEPTH = 3
LANES = 128
TOP = 8
MIB = 1 << 20
TOGETHER = 2


def even_on(axis):
    return lax.rem(lax.axis_index(axis), 2) == 0


def lane_index(rows=8):
    return lax.broadcasted_iota(jnp.int32, (rows, LANES), 1)


def take_lanes(tile, lanes):
    return jnp.take_along_axis(tile, lanes, axis=1)


def pair_exchange(first, second, axis):
    count = lax.axis_size(axis)
    firsts = [(i, i + 1) for i in range(0, count - 1, 2)]
    seconds = [(i, i + 1) for i in range(1, count - 1, 2)]
    got_first = lax.ppermute(first, axis, [p for a, b in firsts for p in ((a, b), (b, a))])
    if not seconds:
        return (got_first,)
    got_second = lax.ppermute(second, axis, [p for a, b in seconds for p in ((a, b), (b, a))])
    return (got_first, got_second)


def pack_faces(rs_ref, k_ref, pad_ref, xa_ref, xb_ref, ya_ref, yb_ref, sems):
    fields = rs_ref.shape[0]
    nx, ny = k_ref.shape[0], k_ref.shape[1]
    copies = [
        pltpu.make_async_copy(
            rs_ref.at[f], pad_ref.at[f, pl.ds(DEPTH, nx), pl.ds(TOP, ny)], sems.at[f]
        )
        for f in range(fields)
    ]
    copies.append(
        pltpu.make_async_copy(
            k_ref, pad_ref.at[fields, pl.ds(DEPTH, nx), pl.ds(TOP, ny)], sems.at[fields]
        )
    )
    for copy in copies:
        copy.start()
    ex, ey = even_on("gx"), even_on("gy")
    start_a = jnp.where(ex, nx, DEPTH)
    start_b = jnp.where(ex, DEPTH, nx)
    for f in range(fields + 1):
        copies[f].wait()
        for i in range(DEPTH):
            xa_ref[f, i] = pad_ref[f, start_a + i, TOP : TOP + ny, :]
            xb_ref[f, i] = pad_ref[f, start_b + i, TOP : TOP + ny, :]
        for x in range(nx):
            low = pad_ref[f, x + DEPTH, TOP : TOP + DEPTH, :]
            high = pad_ref[f, x + DEPTH, TOP + ny - DEPTH : TOP + ny, :]
            row = DEPTH * (f * nx + x)
            ya_ref[row : row + DEPTH, :] = jnp.where(ey, high, low)
            yb_ref[row : row + DEPTH, :] = jnp.where(ey, low, high)


def pack_edges(xa_ref, xb_ref, ea_ref, eb_ref):
    fields, _, ny, _ = xa_ref.shape
    ex, ey = even_on("gx"), even_on("gy")
    for f in range(fields):
        for side in range(2):
            for i in range(DEPTH):
                a, b = xa_ref, xb_ref
                if side == 0:
                    low = jnp.where(ex, b[f, i, :DEPTH, :], a[f, i, :DEPTH, :])
                    high = jnp.where(ex, b[f, i, ny - DEPTH :, :], a[f, i, ny - DEPTH :, :])
                else:
                    low = jnp.where(ex, a[f, i, :DEPTH, :], b[f, i, :DEPTH, :])
                    high = jnp.where(ex, a[f, i, ny - DEPTH :, :], b[f, i, ny - DEPTH :, :])
                row = DEPTH * ((f * 2 + side) * DEPTH + i)
                ea_ref[row : row + DEPTH, :] = jnp.where(ey, high, low)
                eb_ref[row : row + DEPTH, :] = jnp.where(ey, low, high)


def assemble(nx, ny, two_z, pad_in, xa, xb, ya, yb, ea, eb, *outs):
    del pad_in
    if two_z:
        pad, own, za, zb = outs
    else:
        pad, own, za = outs
        zb = None
    slabs = pad.shape[0]
    ex, ey, ez = even_on("gx"), even_on("gy"), even_on("gz")
    bottom = TOP + ny
    wide = nx + 2 * DEPTH
    half = wide // 2
    tiles = (ny + 2 * DEPTH + 7) // 8
    for f in range(slabs):
        for i in range(DEPTH):
            a, b = xa[f, i], xb[f, i]
            pad[f, i, TOP:bottom, :] = jnp.where(ex, b, a)
            pad[f, nx + DEPTH + i, TOP:bottom, :] = jnp.where(ex, a, b)
        for x in range(nx):
            row = DEPTH * (f * nx + x)
            a, b = ya[row : row + DEPTH, :], yb[row : row + DEPTH, :]
            pad[f, x + DEPTH, TOP - DEPTH : TOP, :] = jnp.where(ey, b, a)
            pad[f, x + DEPTH, bottom : bottom + DEPTH, :] = jnp.where(ey, a, b)
        for side in range(2):
            for i in range(DEPTH):
                row = DEPTH * ((f * 2 + side) * DEPTH + i)
                plane = i if side == 0 else nx + DEPTH + i
                a, b = ea[row : row + DEPTH, :], eb[row : row + DEPTH, :]
                pad[f, plane, TOP - DEPTH : TOP, :] = jnp.where(ey, b, a)
                pad[f, plane, bottom : bottom + DEPTH, :] = jnp.where(ey, a, b)

    lane = lane_index()
    place = lane // 2
    is_left = lane % 2 == 1
    column = lane % wide
    step = jnp.minimum(lane // wide, DEPTH - 1)

    def from_halves(first, second, at, zs):
        in_first = at < half
        index = 6 * jnp.where(in_first, at, jnp.minimum(at - half, half - 1)) + zs
        return jnp.where(in_first, take_lanes(first, index), take_lanes(second, index))

    @pl.loop(0, slabs)
    def _(f):
        for t in range(tiles):
            rows = slice(TOP - DEPTH + 8 * t, TOP - DEPTH + 8 * t + 8)
            packed = []
            for part in range(2):
                acc = jnp.zeros((8, LANES), F32)
                for m in range(half):
                    tile = pad[f, part * half + m, rows, :]
                    moved = pltpu.roll(tile, 6 * m + 3, 1)
                    acc = jnp.where(lane // 6 == m, moved, acc)
                packed.append(acc)
            first, second = packed
            out = slice(8 * t, 8 * t + 8)
            for j in range(2):
                own[f, j, out, :] = from_halves(
                    first, second, place, jnp.where(is_left, 3 + j, 2 - j)
                )
            to_left, to_right = 3 + step, 2 - step
            za[f, out, :] = from_halves(first, second, column, jnp.where(ez, to_right, to_left))
            if two_z:
                zb[f, out, :] = from_halves(
                    first, second, column, jnp.where(ez, to_left, to_right)
                )


def face(center, other):
    total = center + other
    return 2.0 * center * other / jnp.where(total > 0, total, 1.0)


def scaled_faces(center, others):
    faces = [face(center, other) for other in others]
    diagonal = faces[0]
    for weight in faces[1:]:
        diagonal = diagonal + weight
    scale = 2.5 / jnp.where(diagonal > 0, diagonal, 1.0)
    return [weight * scale for weight in faces]


def weighted(weights, values):
    accum = weights[0] * values[0]
    for weight, value in zip(weights[1:], values[1:]):
        accum = accum + weight * value
    return accum


def powers(nx, ny, two_z, pad, own, za, *rest):
    if two_z:
        zb, rest = rest[0], rest[1:]
    else:
        zb = None
    high_ref, low_ref, gram_ref, coef, v1, v2, strip, scoef, s1, s2, acc, square = rest
    fields = pad.shape[0] - 1
    wide = nx + 2 * DEPTH
    ez = even_on("gz")
    lane = lane_index()
    place = lane // 2
    is_left = lane % 2 == 1
    tiles = (ny + 2 * DEPTH + 7) // 8

    @pl.loop(0, fields + 1)
    def _(f):
        for t in range(tiles):
            rows = slice(8 * t, 8 * t + 8)
            got_a = za[f, rows, :]
            if two_z:
                got_b = zb[f, rows, :]
                left = jnp.where(ez, got_b, got_a)
                right = jnp.where(ez, got_a, got_b)
            for q in range(DEPTH):
                index = jnp.minimum(wide * (DEPTH - 1 - q) + place, LANES - 1)
                if two_z:
                    tile = jnp.where(is_left, take_lanes(left, index), take_lanes(right, index))
                else:
                    keep = is_left != ez
                    tile = jnp.where(keep, take_lanes(got_a, index), 0.0)
                strip[f, q, rows, :] = tile
            for j in range(2):
                strip[f, DEPTH + j, rows, :] = own[f, j, rows, :]

    def strip_neighbours(ref, f, q, base, row):
        rows = slice(row, row + 8)
        tile = ref[f, q - base, rows, :]
        return tile, [
            pltpu.roll(tile, LANES - 2, 1),
            pltpu.roll(tile, 2, 1),
            ref[f, q - base, row + 1 : row + 9, :],
            ref[f, q - base, row - 1 : row + 7, :],
            ref[f, q + 1 - base, rows, :],
            ref[f, q - 1 - base, rows, :],
        ]

    for q in range(1, 4):
        for t in range(tiles):
            row = 1 + 8 * t
            center, others = strip_neighbours(strip, fields, q, 0, row)
            for n, weight in enumerate(scaled_faces(center, others)):
                scoef[n, q - 1, row : row + 8, :] = weight

    @pl.loop(0, fields)
    def _(f):
        for q in range(1, 4):
            for t in range(tiles):
                row = 1 + 8 * t
                weights = [scoef[n, q - 1, row : row + 8, :] for n in range(6)]
                _, values = strip_neighbours(strip, f, q, 0, row)
                s1[f, q - 1, row : row + 8, :] = weighted(weights, values)
        for t in range(tiles):
            row = 2 + 8 * t
            weights = [scoef[n, 1, row : row + 8, :] for n in range(6)]
            _, values = strip_neighbours(s1, f, 2, 1, row)
            s2[f, row : row + 8, :] = weighted(weights, values)

    def z_pair(tile, edge, plane):
        moved = pltpu.roll(edge, LANES - 1 - 2 * plane, 1)
        return [
            jnp.where(lane == LANES - 1, moved, pltpu.roll(tile, LANES - 1, 1)),
            jnp.where(lane == 0, moved, pltpu.roll(tile, 1, 1)),
        ]

    @pl.loop(0, nx + 4)
    def _(i):
        plane = i + 1
        for t in range(tiles):
            y = 8 * t - 2
            r = TOP + y
            tile = pad[fields, plane, r : r + 8, :]
            others = [
                pad[fields, plane + 1, r : r + 8, :],
                pad[fields, plane - 1, r : r + 8, :],
                pad[fields, plane, r + 1 : r + 9, :],
                pad[fields, plane, r - 1 : r + 7, :],
            ] + z_pair(tile, strip[fields, 2, y + 3 : y + 11, :], plane)
            for n, weight in enumerate(scaled_faces(tile, others)):
                coef[n, i, 8 * t : 8 * t + 8, :] = weight

    def advance(source, source_x, edge, f, plane, y, weights):
        r = TOP + y
        s = plane - source_x
        tile = source[f, s, r : r + 8, :]
        values = [
            source[f, s + 1, r : r + 8, :],
            source[f, s - 1, r : r + 8, :],
            source[f, s, r + 1 : r + 9, :],
            source[f, s, r - 1 : r + 7, :],
        ] + z_pair(tile, edge, plane)
        return weighted(weights, values)

    def weights_at(plane, y):
        return [coef[n, plane - 1, y + 2 : y + 10, :] for n in range(6)]

    def first_power(plane):
        for t in range(tiles):
            y = 8 * t - 2
            weights = weights_at(plane, y)
            for f in range(fields):
                edge = strip[f, 2, y + 3 : y + 11, :]
                v1[f, plane - 1, TOP + y : TOP + y + 8, :] = advance(
                    pad, 0, edge, f, plane, y, weights
                )

    def second_power(plane):
        for t in range(tiles):
            y = 8 * t - 1
            weights = weights_at(plane, y)
            for f in range(fields):
                edge = s1[f, 1, y + 3 : y + 11, :]
                v2[f, plane - 2, TOP + y : TOP + y + 8, :] = advance(
                    v1, 1, edge, f, plane, y, weights
                )

    blocks = ny // 8

    def last_power(plane):
        for t in range(blocks):
            y = 8 * t
            rows = slice(TOP + y, TOP + y + 8)
            weights = weights_at(plane, y)
            columns = [pad[f, plane, rows, :] for f in range(fields)]
            columns += [v1[f, plane - 1, rows, :] for f in range(fields)]
            columns += [v2[f, plane - 2, rows, :] for f in range(fields)]
            for f in range(fields):
                edge = s2[f, y + 3 : y + 11, :]
                columns.append(advance(v2, 2, edge, f, plane, y, weights))
            block = (plane - DEPTH) * blocks + t
            for g in range(len(columns) // 2):
                pair = jnp.concatenate(columns[2 * g : 2 * g + 2], 0)
                high = pair.astype(BF16)
                high_ref[block, 16 * g : 16 * g + 16, :] = high
                low_ref[block, 16 * g : 16 * g + 16, :] = (pair - high.astype(F32)).astype(BF16)

    def products(plane):
        base = (plane - DEPTH) * blocks
        high = jnp.concatenate([high_ref[base + t] for t in range(blocks)], 1)
        low = jnp.concatenate([low_ref[base + t] for t in range(blocks)], 1)
        both = jnp.concatenate([high, low], 0)
        acc[...] += lax.dot_general(
            both, high, (((1,), (1,)), ((), ())), preferred_element_type=F32
        )

    acc[...] = jnp.zeros_like(acc)

    @pl.loop(1, 4)
    def _(plane):
        first_power(plane)

    @pl.loop(4, 7)
    def _(plane):
        second_power(plane - 2)
        first_power(plane)

    last_power(3)
    second_power(5)
    first_power(7)

    @pl.loop(8, nx + 5)
    def _(plane):
        products(plane - 5)
        last_power(plane - 4)
        second_power(plane - 2)
        first_power(plane)

    products(nx)
    last_power(nx + 1)
    second_power(nx + 3)
    products(nx + 1)
    last_power(nx + 2)
    products(nx + 2)

    rows = acc.shape[1]
    sums = acc[...]
    same = lax.broadcasted_iota(jnp.int32, sums.shape, 0) % 8 == (
        lax.broadcasted_iota(jnp.int32, sums.shape, 1) % 8
    )
    sums = jnp.where(same, sums, 0.0).reshape(2 * rows // 8, 8, rows).sum(1)
    pick = lax.broadcasted_iota(jnp.int32, (rows, LANES), 0) // 8 == (
        lax.broadcasted_iota(jnp.int32, (rows, LANES), 1)
    )
    small = jnp.dot(sums, pick.astype(F32), precision=lax.Precision.HIGHEST)
    order = rows // 8
    square[...] = jnp.zeros_like(square)
    square[0:order, :] = small[order : 2 * order, :]
    cross = small[order : 2 * order, :]
    gram_ref[...] = small[0:order, :] + cross + square[...].T[0:order, :]


def factor_and_solve(
    cells, order, nx, ny, gram_a, gram_b, high_ref, low_ref, out_ref, factor_ref, w_wide, w_low, held, sem
):
    blocks = ny // 8
    rows = 8 * order

    row = lax.broadcasted_iota(jnp.int32, (order, LANES), 0)
    lane = lax.broadcasted_iota(jnp.int32, (order, LANES), 1)
    work = (gram_a[...] + gram_b[...]) / cells
    work = jnp.where(lane < order, work, jnp.where(lane == row + 64, 1.0, 0.0))
    for j in range(order):
        pivot = work[j : j + 1, :]
        factor = work[:, j : j + 1] / work[j : j + 1, j : j + 1]
        work = work - jnp.where(row > j, factor * pivot, 0.0)
    pivots = jnp.sum(jnp.where(lane == row, work, 0.0), 1, keepdims=True)
    work = work / jnp.sqrt(pivots)
    factor_ref[...] = jnp.where(lane >= row, work, 0.0)[:, :order]
    inverse = pltpu.roll(work, 64, 1)
    inverse = jnp.where(lane <= row, inverse, 0.0)
    high = inverse.astype(BF16)
    low = (inverse - high.astype(F32)).astype(BF16)
    spread = (
        lax.broadcasted_iota(jnp.int32, (rows, order), 0) // 8
        == lax.broadcasted_iota(jnp.int32, (rows, order), 1)
    ).astype(BF16)
    across = (
        lax.broadcasted_iota(jnp.int32, (LANES, rows), 1) // 8
        == lax.broadcasted_iota(jnp.int32, (LANES, rows), 0)
    ).astype(BF16)
    same = lax.broadcasted_iota(jnp.int32, (rows, rows), 0) % 8 == (
        lax.broadcasted_iota(jnp.int32, (rows, rows), 1) % 8
    )

    def kron(small):
        tall = jnp.dot(spread, small, preferred_element_type=F32).astype(BF16)
        full = jnp.dot(tall, across, preferred_element_type=F32)
        return jnp.where(same, full, 0.0).astype(BF16)

    w_high = kron(high)
    w_wide[:, :rows] = w_high
    w_wide[:, rows:] = w_high
    w_low[...] = kron(low)

    def solve(plane):
        base = plane * blocks
        high = jnp.concatenate([high_ref[base + t] for t in range(blocks)], 1)
        low = jnp.concatenate([low_ref[base + t] for t in range(blocks)], 1)
        both = jnp.concatenate([high, low], 0)
        result = jnp.dot(w_wide[...], both, preferred_element_type=F32)
        result = result + jnp.dot(w_low[...], high, preferred_element_type=F32)
        for t in range(blocks):
            for b in range(order):
                held[b, plane, 8 * t : 8 * t + 8, :] = result[
                    8 * b : 8 * b + 8, LANES * t : LANES * t + LANES
                ]

    def store(step):
        part = pl.ds(step * TOGETHER, TOGETHER)
        return pltpu.make_async_copy(held.at[:, part], out_ref.at[:, part], sem.at[step])

    @pl.loop(0, nx // TOGETHER)
    def _(step):
        for u in range(TOGETHER):
            solve(step * TOGETHER + u)
        store(step).start()

    @pl.loop(0, nx // TOGETHER)
    def _(step):
        store(step).wait()


VM = functools.partial(pl.BlockSpec, memory_space=pltpu.VMEM)


def params(limit):
    return pltpu.CompilerParams(vmem_limit_bytes=limit * MIB)


def on_device(right_sides, permeability):
    fields, nx, ny, nz = right_sides.shape
    slabs = fields + 1
    order = fields * (DEPTH + 1)
    rows = 8 * order
    tall = ny + 16
    wide = nx + 2 * DEPTH
    strip_rows = 8 * ((ny + 2 * DEPTH + 7) // 8)
    two_z = lax.axis_size("gz") > 2
    devices = lax.axis_size("gx") * lax.axis_size("gy") * lax.axis_size("gz")
    cells = float(nx * ny * nz * devices)

    pad_type = pltpu.VMEM((slabs, wide, tall, LANES), F32)
    x_type = pltpu.VMEM((slabs, DEPTH, ny, LANES), F32)
    y_type = pltpu.VMEM((slabs * nx * DEPTH, LANES), F32)
    e_rows = 8 * ((slabs * 2 * DEPTH * DEPTH + 7) // 8)
    e_type = pltpu.VMEM((e_rows, LANES), F32)
    pad, xa, xb, ya, yb = pl.pallas_call(
        pack_faces,
        out_shape=(pad_type, x_type, x_type, y_type, y_type),
        in_specs=[pl.BlockSpec(memory_space=pltpu.HBM)] * 2,
        out_specs=(VM(),) * 5,
        scratch_shapes=[pltpu.SemaphoreType.DMA((slabs,))],
        compiler_params=params(8),
        name="pack_faces",
    )(right_sides, permeability)
    got_xa, got_xb = pair_exchange(xa, xb, "gx")
    got_ya, got_yb = pair_exchange(ya, yb, "gy")
    ea, eb = pl.pallas_call(
        pack_edges,
        out_shape=(e_type, e_type),
        in_specs=[VM()] * 2,
        out_specs=(VM(),) * 2,
        compiler_params=params(8),
        name="pack_edges",
    )(got_xa, got_xb)
    got_ea, got_eb = pair_exchange(ea, eb, "gy")

    own_type = pltpu.VMEM((slabs, 2, strip_rows, LANES), F32)
    z_type = pltpu.VMEM((slabs, strip_rows, LANES), F32)
    z_count = 2 if two_z else 1
    outs = pl.pallas_call(
        functools.partial(assemble, nx, ny, two_z),
        out_shape=(pad_type, own_type) + (z_type,) * z_count,
        in_specs=[VM()] * 7,
        out_specs=(VM(),) * (2 + z_count),
        input_output_aliases={0: 0},
        compiler_params=params(8),
        name="assemble",
    )(pad, got_xa, got_xb, got_ya, got_yb, got_ea, got_eb)
    pad, own = outs[:2]
    got_z = pair_exchange(outs[2], outs[-1], "gz")

    blocks = nx * ny // 8
    split_type = pltpu.VMEM((blocks, rows, LANES), BF16)
    high, low, gram = pl.pallas_call(
        functools.partial(powers, nx, ny, two_z),
        out_shape=(split_type, split_type, pltpu.VMEM((order, LANES), F32)),
        in_specs=[VM()] * (2 + len(got_z)),
        out_specs=(VM(),) * 3,
        scratch_shapes=[
            pltpu.VMEM((6, nx + 4, tall, LANES), F32),
            pltpu.VMEM((fields, nx + 4, tall, LANES), F32),
            pltpu.VMEM((fields, nx + 2, tall, LANES), F32),
            pltpu.VMEM((slabs, 5, tall, LANES), F32),
            pltpu.VMEM((6, 3, tall, LANES), F32),
            pltpu.VMEM((fields, 3, tall, LANES), F32),
            pltpu.VMEM((fields, tall, LANES), F32),
            pltpu.VMEM((2 * rows, rows), F32),
            pltpu.VMEM((LANES, LANES), F32),
        ],
        compiler_params=params(26),
        name="powers",
    )(pad, own, *got_z)

    stages = []
    for axis in ("gz", "gx", "gy"):
        count, stride = lax.axis_size(axis), 1
        while stride < count:
            stages.append((axis, [(i, i ^ stride) for i in range(count)]))
            stride *= 2
    for axis, pairs in stages[:-1]:
        gram = gram + lax.ppermute(gram, axis, pairs)
    other = lax.ppermute(gram, *stages[-1])

    basis_q, factor_r = pl.pallas_call(
        functools.partial(factor_and_solve, cells, order, nx, ny),
        out_shape=(
            jax.ShapeDtypeStruct((order, nx, ny, nz), F32),
            jax.ShapeDtypeStruct((order, order), F32),
        ),
        in_specs=[VM()] * 4,
        out_specs=(pl.BlockSpec(memory_space=pltpu.HBM), VM()),
        scratch_shapes=[
            pltpu.VMEM((rows, 2 * rows), BF16),
            pltpu.VMEM((rows, rows), BF16),
            pltpu.VMEM((order, nx, ny, nz), F32),
            pltpu.SemaphoreType.DMA((nx // TOGETHER,)),
        ],
        compiler_params=params(24),
        name="factor_and_solve",
    )(gram, other, high, low)
    return (basis_q, factor_r)


def solution(mesh):
    placed = (P(None, "gx", "gy", "gz"), P("gx", "gy", "gz"))
    return jax.shard_map(
        on_device,
        mesh=mesh,
        in_specs=placed,
        out_specs=(P(None, "gx", "gy", "gz"), P()),
        check_vma=False,
    )
```

```python
import functools

import jax
import jax.numpy as jnp
from jax import lax
from jax.experimental import pallas as pl
from jax.experimental.pallas import tpu as pltpu
from jax.sharding import PartitionSpec as P

F32 = jnp.float32
BF16 = jnp.bfloat16
DEPTH = 3
LANES = 128
TOP = 8
MIB = 1 << 20
TOGETHER = 2


def even_on(axis):
    return lax.rem(lax.axis_index(axis), 2) == 0


def lane_index(rows=8):
    return lax.broadcasted_iota(jnp.int32, (rows, LANES), 1)


def take_lanes(tile, lanes):
    return jnp.take_along_axis(tile, lanes, axis=1)


def pair_exchange(first, second, axis):
    count = lax.axis_size(axis)
    firsts = [(i, i + 1) for i in range(0, count - 1, 2)]
    seconds = [(i, i + 1) for i in range(1, count - 1, 2)]
    got_first = lax.ppermute(first, axis, [p for a, b in firsts for p in ((a, b), (b, a))])
    if not seconds:
        return (got_first,)
    got_second = lax.ppermute(second, axis, [p for a, b in seconds for p in ((a, b), (b, a))])
    return (got_first, got_second)


def pack_faces(rs_ref, k_ref, pad_ref, xa_ref, xb_ref, ya_ref, yb_ref, sems):
    fields = rs_ref.shape[0]
    nx, ny = k_ref.shape[0], k_ref.shape[1]
    copies = [
        pltpu.make_async_copy(
            rs_ref.at[f], pad_ref.at[f, pl.ds(DEPTH, nx), pl.ds(TOP, ny)], sems.at[f]
        )
        for f in range(fields)
    ]
    copies.append(
        pltpu.make_async_copy(
            k_ref, pad_ref.at[fields, pl.ds(DEPTH, nx), pl.ds(TOP, ny)], sems.at[fields]
        )
    )
    for copy in copies:
        copy.start()
    ex, ey = even_on("gx"), even_on("gy")
    start_a = jnp.where(ex, nx, DEPTH)
    start_b = jnp.where(ex, DEPTH, nx)
    for f in range(fields + 1):
        copies[f].wait()
        for i in range(DEPTH):
            xa_ref[f, i] = pad_ref[f, start_a + i, TOP : TOP + ny, :]
            xb_ref[f, i] = pad_ref[f, start_b + i, TOP : TOP + ny, :]
        for x in range(nx):
            low = pad_ref[f, x + DEPTH, TOP : TOP + DEPTH, :]
            high = pad_ref[f, x + DEPTH, TOP + ny - DEPTH : TOP + ny, :]
            row = DEPTH * (f * nx + x)
            ya_ref[row : row + DEPTH, :] = jnp.where(ey, high, low)
            yb_ref[row : row + DEPTH, :] = jnp.where(ey, low, high)


def pack_edges(xa_ref, xb_ref, ea_ref, eb_ref):
    fields, _, ny, _ = xa_ref.shape
    ex, ey = even_on("gx"), even_on("gy")
    for f in range(fields):
        for side in range(2):
            for i in range(DEPTH):
                a, b = xa_ref, xb_ref
                if side == 0:
                    low = jnp.where(ex, b[f, i, :DEPTH, :], a[f, i, :DEPTH, :])
                    high = jnp.where(ex, b[f, i, ny - DEPTH :, :], a[f, i, ny - DEPTH :, :])
                else:
                    low = jnp.where(ex, a[f, i, :DEPTH, :], b[f, i, :DEPTH, :])
                    high = jnp.where(ex, a[f, i, ny - DEPTH :, :], b[f, i, ny - DEPTH :, :])
                row = DEPTH * ((f * 2 + side) * DEPTH + i)
                ea_ref[row : row + DEPTH, :] = jnp.where(ey, high, low)
                eb_ref[row : row + DEPTH, :] = jnp.where(ey, low, high)


def assemble(nx, ny, two_z, pad_in, inner, xa, xb, ya, yb, ea, eb, *outs):
    del pad_in
    if two_z:
        pad, own, za, zb = outs
    else:
        pad, own, za = outs
        zb = None
    slabs = pad.shape[0]
    ex, ey, ez = even_on("gx"), even_on("gy"), even_on("gz")
    bottom = TOP + ny
    wide = nx + 2 * DEPTH
    half = wide // 2
    tiles = ny // 8 + 1
    for f in range(slabs):
        for i in range(DEPTH):
            a, b = xa[f, i], xb[f, i]
            pad[f, i, TOP:bottom, :] = jnp.where(ex, b, a)
            pad[f, nx + DEPTH + i, TOP:bottom, :] = jnp.where(ex, a, b)
        for x in range(nx):
            row = DEPTH * (f * nx + x)
            a, b = ya[row : row + DEPTH, :], yb[row : row + DEPTH, :]
            pad[f, x + DEPTH, TOP - DEPTH : TOP, :] = jnp.where(ey, b, a)
            pad[f, x + DEPTH, bottom : bottom + DEPTH, :] = jnp.where(ey, a, b)
        for side in range(2):
            for i in range(DEPTH):
                row = DEPTH * ((f * 2 + side) * DEPTH + i)
                plane = i if side == 0 else nx + DEPTH + i
                a, b = ea[row : row + DEPTH, :], eb[row : row + DEPTH, :]
                pad[f, plane, TOP - DEPTH : TOP, :] = jnp.where(ey, b, a)
                pad[f, plane, bottom : bottom + DEPTH, :] = jnp.where(ey, a, b)

    lane = lane_index()
    place = lane // 2
    is_left = lane % 2 == 1
    column = lane % wide
    step = jnp.minimum(lane // wide, DEPTH - 1)
    upper = lax.broadcasted_iota(jnp.int32, (8, LANES), 0) < 4

    def from_halves(first, second, at, zs):
        in_first = at < half
        index = 6 * jnp.where(in_first, at, jnp.minimum(at - half, half - 1)) + zs
        return jnp.where(in_first, take_lanes(first, index), take_lanes(second, index))

    @pl.loop(0, slabs)
    def _(f):
        for t in range(tiles):
            packed = []
            for part in range(2):
                if t < tiles - 1:
                    acc = inner[f, t, part]
                    todo = range(DEPTH) if part == 0 else range(half - DEPTH, half)
                else:
                    acc = jnp.zeros((8, LANES), F32)
                    todo = range(half)
                for m in todo:
                    plane = part * half + m
                    if t < tiles - 1:
                        tile = pad[f, plane, TOP + 8 * t : TOP + 8 * t + 8, :]
                    else:
                        tile = jnp.where(
                            upper,
                            pad[f, plane, TOP - DEPTH : TOP - DEPTH + 8, :],
                            pad[f, plane, bottom - 4 : bottom + 4, :],
                        )
                    acc = jnp.where(lane // 6 == m, pltpu.roll(tile, 6 * m + 3, 1), acc)
                packed.append(acc)
            first, second = packed
            out = slice(8 * t, 8 * t + 8)
            for j in range(2):
                own[f, j, out, :] = from_halves(
                    first, second, place, jnp.where(is_left, 3 + j, 2 - j)
                )
            to_left, to_right = 3 + step, 2 - step
            za[f, out, :] = from_halves(first, second, column, jnp.where(ez, to_right, to_left))
            if two_z:
                zb[f, out, :] = from_halves(
                    first, second, column, jnp.where(ez, to_left, to_right)
                )


def inner_strips(nx, ny, pad, inner):
    half = nx // 2 + DEPTH
    lane = lane_index()

    @pl.loop(0, pad.shape[0])
    def _(f):
        for t in range(ny // 8):
            for part in range(2):
                acc = jnp.zeros((8, LANES), F32)
                for m in range(DEPTH, half) if part == 0 else range(half - DEPTH):
                    tile = pad[f, part * half + m, TOP + 8 * t : TOP + 8 * t + 8, :]
                    acc = jnp.where(lane // 6 == m, pltpu.roll(tile, 6 * m + 3, 1), acc)
                inner[f, t, part] = acc


def face(center, other):
    total = center + other
    return 2.0 * center * other / jnp.where(total > 0, total, 1.0)


def scaled_faces(center, others):
    faces = [face(center, other) for other in others]
    diagonal = faces[0]
    for weight in faces[1:]:
        diagonal = diagonal + weight
    scale = 2.5 / jnp.where(diagonal > 0, diagonal, 1.0)
    return [weight * scale for weight in faces]


def weighted(weights, values):
    accum = weights[0] * values[0]
    for weight, value in zip(weights[1:], values[1:]):
        accum = accum + weight * value
    return accum


def powers(nx, ny, two_z, pad, own, za, *rest):
    if two_z:
        zb, rest = rest[0], rest[1:]
    else:
        zb = None
    high_ref, low_ref, gram_ref, coef, v1, v2, strip, scoef, s1, s2, acc, square = rest
    fields = pad.shape[0] - 1
    wide = nx + 2 * DEPTH
    ez = even_on("gz")
    lane = lane_index()
    place = lane // 2
    is_left = lane % 2 == 1
    tiles = (ny + 2 * DEPTH + 7) // 8

    @pl.loop(0, fields + 1)
    def _(f):
        def put(q, t, tile):
            if t < ny // 8:
                strip[f, q, DEPTH + 8 * t : DEPTH + 8 * t + 8, :] = tile
            else:
                strip[f, q, 0:DEPTH, :] = tile[0:DEPTH, :]
                strip[f, q, DEPTH + ny : 2 * DEPTH + ny, :] = tile[4 : 4 + DEPTH, :]

        for t in range(ny // 8 + 1):
            rows = slice(8 * t, 8 * t + 8)
            got_a = za[f, rows, :]
            if two_z:
                got_b = zb[f, rows, :]
                left = jnp.where(ez, got_b, got_a)
                right = jnp.where(ez, got_a, got_b)
            for q in range(DEPTH):
                index = jnp.minimum(wide * (DEPTH - 1 - q) + place, LANES - 1)
                if two_z:
                    tile = jnp.where(is_left, take_lanes(left, index), take_lanes(right, index))
                else:
                    keep = is_left != ez
                    tile = jnp.where(keep, take_lanes(got_a, index), 0.0)
                put(q, t, tile)
            for j in range(2):
                put(DEPTH + j, t, own[f, j, rows, :])

    def strip_neighbours(ref, f, q, base, row):
        rows = slice(row, row + 8)
        tile = ref[f, q - base, rows, :]
        return tile, [
            pltpu.roll(tile, LANES - 2, 1),
            pltpu.roll(tile, 2, 1),
            ref[f, q - base, row + 1 : row + 9, :],
            ref[f, q - base, row - 1 : row + 7, :],
            ref[f, q + 1 - base, rows, :],
            ref[f, q - 1 - base, rows, :],
        ]

    for q in range(1, 4):
        for t in range(tiles):
            row = 1 + 8 * t
            center, others = strip_neighbours(strip, fields, q, 0, row)
            for n, weight in enumerate(scaled_faces(center, others)):
                scoef[n, q - 1, row : row + 8, :] = weight

    @pl.loop(0, fields)
    def _(f):
        for q in range(1, 4):
            for t in range(tiles):
                row = 1 + 8 * t
                weights = [scoef[n, q - 1, row : row + 8, :] for n in range(6)]
                _, values = strip_neighbours(strip, f, q, 0, row)
                s1[f, q - 1, row : row + 8, :] = weighted(weights, values)
        for t in range(tiles):
            row = 2 + 8 * t
            weights = [scoef[n, 1, row : row + 8, :] for n in range(6)]
            _, values = strip_neighbours(s1, f, 2, 1, row)
            s2[f, row : row + 8, :] = weighted(weights, values)

    def z_pair(tile, edge, plane):
        moved = pltpu.roll(edge, LANES - 1 - 2 * plane, 1)
        return [
            jnp.where(lane == LANES - 1, moved, pltpu.roll(tile, LANES - 1, 1)),
            jnp.where(lane == 0, moved, pltpu.roll(tile, 1, 1)),
        ]

    @pl.loop(0, nx + 4)
    def _(i):
        plane = i + 1
        for t in range(tiles):
            y = 8 * t - 2
            r = TOP + y
            tile = pad[fields, plane, r : r + 8, :]
            others = [
                pad[fields, plane + 1, r : r + 8, :],
                pad[fields, plane - 1, r : r + 8, :],
                pad[fields, plane, r + 1 : r + 9, :],
                pad[fields, plane, r - 1 : r + 7, :],
            ] + z_pair(tile, strip[fields, 2, y + 3 : y + 11, :], plane)
            for n, weight in enumerate(scaled_faces(tile, others)):
                coef[n, i, 8 * t : 8 * t + 8, :] = weight

    def advance(source, source_x, edge, f, plane, y, weights):
        r = TOP + y
        s = plane - source_x
        tile = source[f, s, r : r + 8, :]
        values = [
            source[f, s + 1, r : r + 8, :],
            source[f, s - 1, r : r + 8, :],
            source[f, s, r + 1 : r + 9, :],
            source[f, s, r - 1 : r + 7, :],
        ] + z_pair(tile, edge, plane)
        return weighted(weights, values)

    def weights_at(plane, y):
        return [coef[n, plane - 1, y + 2 : y + 10, :] for n in range(6)]

    def first_power(plane):
        for t in range(tiles):
            y = 8 * t - 2
            weights = weights_at(plane, y)
            for f in range(fields):
                edge = strip[f, 2, y + 3 : y + 11, :]
                v1[f, plane - 1, TOP + y : TOP + y + 8, :] = advance(
                    pad, 0, edge, f, plane, y, weights
                )

    def second_power(plane):
        for t in range(tiles):
            y = 8 * t - 1
            weights = weights_at(plane, y)
            for f in range(fields):
                edge = s1[f, 1, y + 3 : y + 11, :]
                v2[f, plane - 2, TOP + y : TOP + y + 8, :] = advance(
                    v1, 1, edge, f, plane, y, weights
                )

    blocks = ny // 8

    def last_power(plane):
        for t in range(blocks):
            y = 8 * t
            rows = slice(TOP + y, TOP + y + 8)
            weights = weights_at(plane, y)
            columns = [pad[f, plane, rows, :] for f in range(fields)]
            columns += [v1[f, plane - 1, rows, :] for f in range(fields)]
            columns += [v2[f, plane - 2, rows, :] for f in range(fields)]
            for f in range(fields):
                edge = s2[f, y + 3 : y + 11, :]
                columns.append(advance(v2, 2, edge, f, plane, y, weights))
            block = (plane - DEPTH) * blocks + t
            for g in range(len(columns) // 2):
                pair = jnp.concatenate(columns[2 * g : 2 * g + 2], 0)
                high = pair.astype(BF16)
                high_ref[block, 16 * g : 16 * g + 16, :] = high
                low_ref[block, 16 * g : 16 * g + 16, :] = (pair - high.astype(F32)).astype(BF16)

    def products(plane):
        base = (plane - DEPTH) * blocks
        high = jnp.concatenate([high_ref[base + t] for t in range(blocks)], 1)
        low = jnp.concatenate([low_ref[base + t] for t in range(blocks)], 1)
        both = jnp.concatenate([high, low], 0)
        acc[...] += lax.dot_general(
            both, high, (((1,), (1,)), ((), ())), preferred_element_type=F32
        )

    acc[...] = jnp.zeros_like(acc)

    @pl.loop(1, 4)
    def _(plane):
        first_power(plane)

    @pl.loop(4, 7)
    def _(plane):
        second_power(plane - 2)
        first_power(plane)

    last_power(3)
    second_power(5)
    first_power(7)

    @pl.loop(8, nx + 5)
    def _(plane):
        products(plane - 5)
        last_power(plane - 4)
        second_power(plane - 2)
        first_power(plane)

    products(nx)
    last_power(nx + 1)
    second_power(nx + 3)
    products(nx + 1)
    last_power(nx + 2)
    products(nx + 2)

    rows = acc.shape[1]
    sums = acc[...]
    same = lax.broadcasted_iota(jnp.int32, sums.shape, 0) % 8 == (
        lax.broadcasted_iota(jnp.int32, sums.shape, 1) % 8
    )
    sums = jnp.where(same, sums, 0.0).reshape(2 * rows // 8, 8, rows).sum(1)
    pick = lax.broadcasted_iota(jnp.int32, (rows, LANES), 0) // 8 == (
        lax.broadcasted_iota(jnp.int32, (rows, LANES), 1)
    )
    small = jnp.dot(sums, pick.astype(F32), precision=lax.Precision.HIGHEST)
    order = rows // 8
    square[...] = jnp.zeros_like(square)
    square[0:order, :] = small[order : 2 * order, :]
    cross = small[order : 2 * order, :]
    gram_ref[...] = small[0:order, :] + cross + square[...].T[0:order, :]


def factor_and_solve(
    cells, order, nx, ny, gram_a, gram_b, high_ref, low_ref, out_ref, factor_ref, w_wide, w_low, held, sem
):
    blocks = ny // 8
    rows = 8 * order

    row = lax.broadcasted_iota(jnp.int32, (order, LANES), 0)
    lane = lax.broadcasted_iota(jnp.int32, (order, LANES), 1)
    work = (gram_a[...] + gram_b[...]) / cells
    work = jnp.where(lane < order, work, jnp.where(lane == row + 64, 1.0, 0.0))
    for start in range(0, order, 8):
        columns = [
            jnp.broadcast_to(work[:, j : j + 1], (order, LANES)) for j in range(start, start + 8)
        ]
        for k in range(8):
            j = start + k
            factor = jnp.where(row > j, columns[k] / columns[k][j : j + 1, :], 0.0)
            work = work - factor * work[j : j + 1, :]
            for m in range(k + 1, 8):
                columns[m] = columns[m] - factor * columns[m][j : j + 1, :]
    pivots = jnp.sum(jnp.where(lane == row, work, 0.0), 1, keepdims=True)
    work = work / jnp.sqrt(pivots)
    factor_ref[...] = jnp.where(lane >= row, work, 0.0)[:, :order]
    inverse = pltpu.roll(work, 64, 1)
    inverse = jnp.where(lane <= row, inverse, 0.0)
    high = inverse.astype(BF16)
    low = (inverse - high.astype(F32)).astype(BF16)
    spread = (
        lax.broadcasted_iota(jnp.int32, (rows, order), 0) // 8
        == lax.broadcasted_iota(jnp.int32, (rows, order), 1)
    ).astype(BF16)
    across = (
        lax.broadcasted_iota(jnp.int32, (LANES, rows), 1) // 8
        == lax.broadcasted_iota(jnp.int32, (LANES, rows), 0)
    ).astype(BF16)
    same = lax.broadcasted_iota(jnp.int32, (rows, rows), 0) % 8 == (
        lax.broadcasted_iota(jnp.int32, (rows, rows), 1) % 8
    )

    def kron(small):
        tall = jnp.dot(spread, small, preferred_element_type=F32).astype(BF16)
        full = jnp.dot(tall, across, preferred_element_type=F32)
        return jnp.where(same, full, 0.0).astype(BF16)

    w_high = kron(high)
    w_wide[:, :rows] = w_high
    w_wide[:, rows:] = w_high
    w_low[...] = kron(low)

    def solve(plane):
        base = plane * blocks
        high = jnp.concatenate([high_ref[base + t] for t in range(blocks)], 1)
        low = jnp.concatenate([low_ref[base + t] for t in range(blocks)], 1)
        both = jnp.concatenate([high, low], 0)
        result = jnp.dot(w_wide[...], both, preferred_element_type=F32)
        result = result + jnp.dot(w_low[...], high, preferred_element_type=F32)
        for t in range(blocks):
            for b in range(order):
                held[b, plane, 8 * t : 8 * t + 8, :] = result[
                    8 * b : 8 * b + 8, LANES * t : LANES * t + LANES
                ]

    def store(step):
        part = pl.ds(step * TOGETHER, TOGETHER)
        return pltpu.make_async_copy(held.at[:, part], out_ref.at[:, part], sem.at[step])

    @pl.loop(0, nx // TOGETHER)
    def _(step):
        for u in range(TOGETHER):
            solve(step * TOGETHER + u)
        store(step).start()

    @pl.loop(0, nx // TOGETHER)
    def _(step):
        store(step).wait()


VM = functools.partial(pl.BlockSpec, memory_space=pltpu.VMEM)


def params(limit):
    return pltpu.CompilerParams(vmem_limit_bytes=limit * MIB)


def on_device(right_sides, permeability):
    fields, nx, ny, nz = right_sides.shape
    slabs = fields + 1
    order = fields * (DEPTH + 1)
    rows = 8 * order
    tall = ny + 16
    wide = nx + 2 * DEPTH
    strip_rows = ny + 8
    two_z = lax.axis_size("gz") > 2
    devices = lax.axis_size("gx") * lax.axis_size("gy") * lax.axis_size("gz")
    cells = float(nx * ny * nz * devices)

    pad_type = pltpu.VMEM((slabs, wide, tall, LANES), F32)
    x_type = pltpu.VMEM((slabs, DEPTH, ny, LANES), F32)
    y_type = pltpu.VMEM((slabs * nx * DEPTH, LANES), F32)
    e_rows = 8 * ((slabs * 2 * DEPTH * DEPTH + 7) // 8)
    e_type = pltpu.VMEM((e_rows, LANES), F32)
    pad, xa, xb, ya, yb = pl.pallas_call(
        pack_faces,
        out_shape=(pad_type, x_type, x_type, y_type, y_type),
        in_specs=[pl.BlockSpec(memory_space=pltpu.HBM)] * 2,
        out_specs=(VM(),) * 5,
        scratch_shapes=[pltpu.SemaphoreType.DMA((slabs,))],
        compiler_params=params(46),
        name="pack_faces",
    )(right_sides, permeability)
    got_ya, got_yb = pair_exchange(ya, yb, "gy")
    got_xa, got_xb = pair_exchange(xa, xb, "gx")
    inner = pl.pallas_call(
        functools.partial(inner_strips, nx, ny),
        out_shape=pltpu.VMEM((slabs, ny // 8, 2, 8, LANES), F32),
        in_specs=[VM()],
        out_specs=VM(),
        compiler_params=params(8),
        name="inner_strips",
        cost_estimate=pl.CostEstimate(flops=slabs * nx * ny * nz * 200, bytes_accessed=4 * slabs * nx * ny * nz, transcendentals=0),
    )(pad)
    ea, eb = pl.pallas_call(
        pack_edges,
        out_shape=(e_type, e_type),
        in_specs=[VM()] * 2,
        out_specs=(VM(),) * 2,
        compiler_params=params(8),
        name="pack_edges",
    )(got_xa, got_xb)
    got_ea, got_eb = pair_exchange(ea, eb, "gy")

    own_type = pltpu.VMEM((slabs, 2, strip_rows, LANES), F32)
    z_type = pltpu.VMEM((slabs, strip_rows, LANES), F32)
    z_count = 2 if two_z else 1
    outs = pl.pallas_call(
        functools.partial(assemble, nx, ny, two_z),
        out_shape=(pad_type, own_type) + (z_type,) * z_count,
        in_specs=[VM()] * 8,
        out_specs=(VM(),) * (2 + z_count),
        input_output_aliases={0: 0},
        compiler_params=params(8),
        name="assemble",
    )(pad, inner, got_xa, got_xb, got_ya, got_yb, got_ea, got_eb)
    pad, own = outs[:2]
    got_z = pair_exchange(outs[2], outs[-1], "gz")

    blocks = nx * ny // 8
    split_type = pltpu.VMEM((blocks, rows, LANES), BF16)
    high, low, gram = pl.pallas_call(
        functools.partial(powers, nx, ny, two_z),
        out_shape=(split_type, split_type, pltpu.VMEM((order, LANES), F32)),
        in_specs=[VM()] * (2 + len(got_z)),
        out_specs=(VM(),) * 3,
        scratch_shapes=[
            pltpu.VMEM((6, nx + 4, tall, LANES), F32),
            pltpu.VMEM((fields, nx + 4, tall, LANES), F32),
            pltpu.VMEM((fields, nx + 2, tall, LANES), F32),
            pltpu.VMEM((slabs, 5, tall, LANES), F32),
            pltpu.VMEM((6, 3, tall, LANES), F32),
            pltpu.VMEM((fields, 3, tall, LANES), F32),
            pltpu.VMEM((fields, tall, LANES), F32),
            pltpu.VMEM((2 * rows, rows), F32),
            pltpu.VMEM((LANES, LANES), F32),
        ],
        compiler_params=params(26),
        name="powers",
    )(pad, own, *got_z)

    stages = []
    for axis in ("gz", "gx", "gy"):
        count, stride = lax.axis_size(axis), 1
        while stride < count:
            stages.append((axis, [(i, i ^ stride) for i in range(count)]))
            stride *= 2
    for axis, pairs in stages[:-1]:
        gram = gram + lax.ppermute(gram, axis, pairs)
    other = lax.ppermute(gram, *stages[-1])

    basis_q, factor_r = pl.pallas_call(
        functools.partial(factor_and_solve, cells, order, nx, ny),
        out_shape=(
            jax.ShapeDtypeStruct((order, nx, ny, nz), F32),
            jax.ShapeDtypeStruct((order, order), F32),
        ),
        in_specs=[VM()] * 4,
        out_specs=(pl.BlockSpec(memory_space=pltpu.HBM), VM()),
        scratch_shapes=[
            pltpu.VMEM((rows, 2 * rows), BF16),
            pltpu.VMEM((rows, rows), BF16),
            pltpu.VMEM((order, nx, ny, nz), F32),
            pltpu.SemaphoreType.DMA((nx // TOGETHER,)),
        ],
        compiler_params=params(24),
        name="factor_and_solve",
    )(gram, other, high, low)
    return (basis_q, factor_r)


def solution(mesh):
    placed = (P(None, "gx", "gy", "gz"), P("gx", "gy", "gz"))
    return jax.shard_map(
        on_device,
        mesh=mesh,
        in_specs=placed,
        out_specs=(P(None, "gx", "gy", "gz"), P()),
        check_vma=False,
    )
```

```python
import functools

import jax
import jax.numpy as jnp
from jax import lax
from jax.experimental import pallas as pl
from jax.experimental.pallas import tpu as pltpu
from jax.sharding import PartitionSpec as P

F32 = jnp.float32
BF16 = jnp.bfloat16
DEPTH = 3
LANES = 128
TOP = 8
MIB = 1 << 20
TOGETHER = 4


def even_on(axis):
    return lax.rem(lax.axis_index(axis), 2) == 0


def lane_index(rows=8):
    return lax.broadcasted_iota(jnp.int32, (rows, LANES), 1)


def take_lanes(tile, lanes):
    return jnp.take_along_axis(tile, lanes, axis=1)


def pair_exchange(first, second, axis):
    count = lax.axis_size(axis)
    firsts = [(i, i + 1) for i in range(0, count - 1, 2)]
    seconds = [(i, i + 1) for i in range(1, count - 1, 2)]
    got_first = lax.ppermute(first, axis, [p for a, b in firsts for p in ((a, b), (b, a))])
    if not seconds:
        return (got_first,)
    got_second = lax.ppermute(second, axis, [p for a, b in seconds for p in ((a, b), (b, a))])
    return (got_first, got_second)


def pack_faces(rs_ref, k_ref, pad_ref, xa_ref, xb_ref, ya_ref, yb_ref, sems):
    fields = rs_ref.shape[0]
    nx, ny = k_ref.shape[0], k_ref.shape[1]
    copies = [
        pltpu.make_async_copy(
            rs_ref.at[f], pad_ref.at[f, pl.ds(DEPTH, nx), pl.ds(TOP, ny)], sems.at[f]
        )
        for f in range(fields)
    ]
    copies.append(
        pltpu.make_async_copy(
            k_ref, pad_ref.at[fields, pl.ds(DEPTH, nx), pl.ds(TOP, ny)], sems.at[fields]
        )
    )
    for copy in copies:
        copy.start()
    ex, ey = even_on("gx"), even_on("gy")
    start_a = jnp.where(ex, nx, DEPTH)
    start_b = jnp.where(ex, DEPTH, nx)
    for f in range(fields + 1):
        copies[f].wait()
        for i in range(DEPTH):
            xa_ref[f, i] = pad_ref[f, start_a + i, TOP : TOP + ny, :]
            xb_ref[f, i] = pad_ref[f, start_b + i, TOP : TOP + ny, :]
        for x in range(nx):
            low = pad_ref[f, x + DEPTH, TOP : TOP + DEPTH, :]
            high = pad_ref[f, x + DEPTH, TOP + ny - DEPTH : TOP + ny, :]
            row = DEPTH * (f * nx + x)
            ya_ref[row : row + DEPTH, :] = jnp.where(ey, high, low)
            yb_ref[row : row + DEPTH, :] = jnp.where(ey, low, high)


def pack_edges(xa_ref, xb_ref, ea_ref, eb_ref):
    fields, _, ny, _ = xa_ref.shape
    ex, ey = even_on("gx"), even_on("gy")
    for f in range(fields):
        for side in range(2):
            for i in range(DEPTH):
                a, b = xa_ref, xb_ref
                if side == 0:
                    low = jnp.where(ex, b[f, i, :DEPTH, :], a[f, i, :DEPTH, :])
                    high = jnp.where(ex, b[f, i, ny - DEPTH :, :], a[f, i, ny - DEPTH :, :])
                else:
                    low = jnp.where(ex, a[f, i, :DEPTH, :], b[f, i, :DEPTH, :])
                    high = jnp.where(ex, a[f, i, ny - DEPTH :, :], b[f, i, ny - DEPTH :, :])
                row = DEPTH * ((f * 2 + side) * DEPTH + i)
                ea_ref[row : row + DEPTH, :] = jnp.where(ey, high, low)
                eb_ref[row : row + DEPTH, :] = jnp.where(ey, low, high)


def assemble(nx, ny, two_z, pad_in, inner, xa, xb, ya, yb, ea, eb, *outs):
    del pad_in
    if two_z:
        pad, own, za, zb = outs
    else:
        pad, own, za = outs
        zb = None
    slabs = pad.shape[0]
    ex, ey, ez = even_on("gx"), even_on("gy"), even_on("gz")
    bottom = TOP + ny
    wide = nx + 2 * DEPTH
    half = wide // 2
    tiles = ny // 8 + 1
    for f in range(slabs):
        for i in range(DEPTH):
            a, b = xa[f, i], xb[f, i]
            pad[f, i, TOP:bottom, :] = jnp.where(ex, b, a)
            pad[f, nx + DEPTH + i, TOP:bottom, :] = jnp.where(ex, a, b)
        for x in range(nx):
            row = DEPTH * (f * nx + x)
            a, b = ya[row : row + DEPTH, :], yb[row : row + DEPTH, :]
            pad[f, x + DEPTH, TOP - DEPTH : TOP, :] = jnp.where(ey, b, a)
            pad[f, x + DEPTH, bottom : bottom + DEPTH, :] = jnp.where(ey, a, b)
        for side in range(2):
            for i in range(DEPTH):
                row = DEPTH * ((f * 2 + side) * DEPTH + i)
                plane = i if side == 0 else nx + DEPTH + i
                a, b = ea[row : row + DEPTH, :], eb[row : row + DEPTH, :]
                pad[f, plane, TOP - DEPTH : TOP, :] = jnp.where(ey, b, a)
                pad[f, plane, bottom : bottom + DEPTH, :] = jnp.where(ey, a, b)

    lane = lane_index()
    place = lane // 2
    is_left = lane % 2 == 1
    column = lane % wide
    step = jnp.minimum(lane // wide, DEPTH - 1)
    upper = lax.broadcasted_iota(jnp.int32, (8, LANES), 0) < 4

    def from_halves(first, second, at, zs):
        in_first = at < half
        index = 6 * jnp.where(in_first, at, jnp.minimum(at - half, half - 1)) + zs
        return jnp.where(in_first, take_lanes(first, index), take_lanes(second, index))

    @pl.loop(0, slabs)
    def _(f):
        for t in range(tiles):
            packed = []
            for part in range(2):
                if t < tiles - 1:
                    acc = inner[f, t, part]
                    todo = range(DEPTH) if part == 0 else range(half - DEPTH, half)
                else:
                    acc = jnp.zeros((8, LANES), F32)
                    todo = range(half)
                for m in todo:
                    plane = part * half + m
                    if t < tiles - 1:
                        tile = pad[f, plane, TOP + 8 * t : TOP + 8 * t + 8, :]
                    else:
                        tile = jnp.where(
                            upper,
                            pad[f, plane, TOP - DEPTH : TOP - DEPTH + 8, :],
                            pad[f, plane, bottom - 4 : bottom + 4, :],
                        )
                    acc = jnp.where(lane // 6 == m, pltpu.roll(tile, 6 * m + 3, 1), acc)
                packed.append(acc)
            first, second = packed
            out = slice(8 * t, 8 * t + 8)
            for j in range(2):
                own[f, j, out, :] = from_halves(
                    first, second, place, jnp.where(is_left, 3 + j, 2 - j)
                )
            to_left, to_right = 3 + step, 2 - step
            za[f, out, :] = from_halves(first, second, column, jnp.where(ez, to_right, to_left))
            if two_z:
                zb[f, out, :] = from_halves(
                    first, second, column, jnp.where(ez, to_left, to_right)
                )


def inner_strips(nx, ny, pad, inner):
    half = nx // 2 + DEPTH
    lane = lane_index()

    @pl.loop(0, pad.shape[0])
    def _(f):
        for t in range(ny // 8):
            for part in range(2):
                acc = jnp.zeros((8, LANES), F32)
                for m in range(DEPTH, half) if part == 0 else range(half - DEPTH):
                    tile = pad[f, part * half + m, TOP + 8 * t : TOP + 8 * t + 8, :]
                    acc = jnp.where(lane // 6 == m, pltpu.roll(tile, 6 * m + 3, 1), acc)
                inner[f, t, part] = acc


def face(center, other):
    total = center + other
    return 2.0 * center * other / jnp.where(total > 0, total, 1.0)


def plane_faces(nx, ny, pad, faces):
    fields = pad.shape[0] - 1
    lane = lane_index()

    @pl.loop(0, nx + 4, unroll=2)
    def _(i):
        plane = i + 1
        for t in range((ny + 2 * DEPTH + 7) // 8):
            r = TOP - 2 + 8 * t
            tile = pad[fields, plane, r : r + 8, :]
            beside = face(tile, pltpu.roll(tile, LANES - 1, 1))
            beside = jnp.where(lane == LANES - 1, 0.0, beside)
            found = [
                face(tile, pad[fields, plane + 1, r : r + 8, :]),
                face(tile, pad[fields, plane - 1, r : r + 8, :]),
                face(tile, pad[fields, plane, r + 1 : r + 9, :]),
                face(tile, pad[fields, plane, r - 1 : r + 7, :]),
                beside,
                pltpu.roll(beside, 1, 1),
            ]
            for n, weight in enumerate(found):
                faces[n, i, 8 * t : 8 * t + 8, :] = weight


def scaled_faces(center, others):
    faces = [face(center, other) for other in others]
    diagonal = faces[0]
    for weight in faces[1:]:
        diagonal = diagonal + weight
    scale = 2.5 / jnp.where(diagonal > 0, diagonal, 1.0)
    return [weight * scale for weight in faces]


def weighted(weights, values):
    accum = weights[0] * values[0]
    for weight, value in zip(weights[1:], values[1:]):
        accum = accum + weight * value
    return accum


def powers(nx, ny, two_z, pad, own, faces, za, *rest):
    if two_z:
        zb, rest = rest[0], rest[1:]
    else:
        zb = None
    high_ref, low_ref, gram_ref, coef, v1, v2, strip, scoef, s1, s2, acc, square, edge = rest
    fields = pad.shape[0] - 1
    wide = nx + 2 * DEPTH
    ez = even_on("gz")
    lane = lane_index()
    place = lane // 2
    is_left = lane % 2 == 1
    tiles = (ny + 2 * DEPTH + 7) // 8

    @pl.loop(0, fields + 1)
    def _(f):
        def put(q, t, tile):
            if t < ny // 8:
                strip[f, q, DEPTH + 8 * t : DEPTH + 8 * t + 8, :] = tile
            else:
                strip[f, q, 0:DEPTH, :] = tile[0:DEPTH, :]
                strip[f, q, DEPTH + ny : 2 * DEPTH + ny, :] = tile[4 : 4 + DEPTH, :]

        for t in range(ny // 8 + 1):
            rows = slice(8 * t, 8 * t + 8)
            got_a = za[f, rows, :]
            if two_z:
                got_b = zb[f, rows, :]
                left = jnp.where(ez, got_b, got_a)
                right = jnp.where(ez, got_a, got_b)
            for q in range(DEPTH):
                index = jnp.minimum(wide * (DEPTH - 1 - q) + place, LANES - 1)
                if two_z:
                    tile = jnp.where(is_left, take_lanes(left, index), take_lanes(right, index))
                else:
                    keep = is_left != ez
                    tile = jnp.where(keep, take_lanes(got_a, index), 0.0)
                put(q, t, tile)
            for j in range(2):
                put(DEPTH + j, t, own[f, j, rows, :])

    def strip_neighbours(ref, f, q, base, row):
        rows = slice(row, row + 8)
        tile = ref[f, q - base, rows, :]
        return tile, [
            pltpu.roll(tile, LANES - 2, 1),
            pltpu.roll(tile, 2, 1),
            ref[f, q - base, row + 1 : row + 9, :],
            ref[f, q - base, row - 1 : row + 7, :],
            ref[f, q + 1 - base, rows, :],
            ref[f, q - 1 - base, rows, :],
        ]

    for q in range(1, 4):
        for t in range(tiles):
            row = 1 + 8 * t
            center, others = strip_neighbours(strip, fields, q, 0, row)
            for n, weight in enumerate(scaled_faces(center, others)):
                scoef[n, q - 1, row : row + 8, :] = weight

    @pl.loop(0, fields)
    def _(f):
        for q in range(1, 4):
            for t in range(tiles):
                row = 1 + 8 * t
                weights = [scoef[n, q - 1, row : row + 8, :] for n in range(6)]
                _, values = strip_neighbours(strip, f, q, 0, row)
                s1[f, q - 1, row : row + 8, :] = weighted(weights, values)
        for t in range(tiles):
            row = 2 + 8 * t
            weights = [scoef[n, 1, row : row + 8, :] for n in range(6)]
            _, values = strip_neighbours(s1, f, 2, 1, row)
            s2[f, row : row + 8, :] = weighted(weights, values)

    def fill(base, count, y, lag, values_at):
        for t in range(count):
            row = y + DEPTH + 8 * t
            weight = scoef[5, 2, row : row + 8, :]
            for g in range(fields // 2):
                pair = [
                    pltpu.roll(weight * values_at(f, slice(row, row + 8)), 2 * lag, 1)
                    if lag
                    else weight * values_at(f, slice(row, row + 8))
                    for f in (2 * g, 2 * g + 1)
                ]
                pair = jnp.concatenate(pair, 0)
                high = pair.astype(BF16)
                at = base + 8 * (t * fields + 2 * g)
                edge[at : at + 16, :LANES] = high
                edge[at : at + 16, LANES:] = (pair - high.astype(F32)).astype(BF16)

    base2 = fields * ny
    base1 = base2 + 8 * fields * tiles
    ends = base1 + 8 * fields * tiles
    fill(0, ny // 8, 0, 4, lambda f, rows: s2[f, rows, :])
    fill(base2, tiles, -1, 2, lambda f, rows: s1[f, 1, rows, :])
    fill(base1, tiles, -2, 0, lambda f, rows: strip[f, 2, rows, :])

    def chosen(front):
        lanes = lane_index(LANES)
        source = jnp.where(
            lanes == 0, 2 * front + 1, jnp.where(lanes == LANES - 1, 2 * front, -1)
        )
        one_hot = lax.broadcasted_iota(jnp.int32, (LANES, LANES), 0) == source
        one_hot = jnp.where(one_hot, 1.0, 0.0).astype(BF16)
        return jnp.concatenate([one_hot, one_hot], 0)

    def beyond(front, start, stop):
        return jnp.dot(edge[start:stop, :], chosen(front), preferred_element_type=F32)

    @pl.loop(0, nx + 4, unroll=4)
    def _(i):
        plane = i + 1
        for t in range(tiles):
            y = 8 * t - 2
            tile = pad[fields, plane, TOP + y : TOP + y + 8, :]
            outside = pltpu.roll(strip[fields, 2, y + 3 : y + 11, :], LANES - 1 - 2 * plane, 1)
            weights = [faces[n, i, 8 * t : 8 * t + 8, :] for n in range(6)]
            diagonal = jnp.where(
                (lane == 0) | (lane == LANES - 1), face(tile, outside), 0.0
            )
            for weight in weights:
                diagonal = diagonal + weight
            scale = 2.5 / jnp.where(diagonal > 0, diagonal, 1.0)
            for n, weight in enumerate(weights):
                coef[n, i, 8 * t : 8 * t + 8, :] = weight * scale

    def advance(source, source_x, extra, f, plane, y, weights):
        r = TOP + y
        s = plane - source_x
        tile = source[f, s, r : r + 8, :]
        values = [
            source[f, s + 1, r : r + 8, :],
            source[f, s - 1, r : r + 8, :],
            source[f, s, r + 1 : r + 9, :],
            source[f, s, r - 1 : r + 7, :],
            pltpu.roll(tile, LANES - 1, 1),
            pltpu.roll(tile, 1, 1),
        ]
        return weighted(weights, values) + extra

    def weights_at(plane, y):
        return [coef[n, plane - 1, y + 2 : y + 10, :] for n in range(6)]

    def extra_of(terms, t, f):
        at = 8 * (t * fields + f)
        return terms[at : at + 8, :]

    def first_power(plane, terms):
        for t in range(tiles):
            y = 8 * t - 2
            weights = weights_at(plane, y)
            for f in range(fields):
                v1[f, plane - 1, TOP + y : TOP + y + 8, :] = advance(
                    pad, 0, extra_of(terms, t, f), f, plane, y, weights
                )

    def second_power(plane, terms):
        for t in range(tiles):
            y = 8 * t - 1
            weights = weights_at(plane, y)
            for f in range(fields):
                v2[f, plane - 2, TOP + y : TOP + y + 8, :] = advance(
                    v1, 1, extra_of(terms, t, f), f, plane, y, weights
                )

    blocks = ny // 8

    def last_power(plane, terms):
        for t in range(blocks):
            y = 8 * t
            rows = slice(TOP + y, TOP + y + 8)
            weights = weights_at(plane, y)
            columns = [pad[f, plane, rows, :] for f in range(fields)]
            columns += [v1[f, plane - 1, rows, :] for f in range(fields)]
            columns += [v2[f, plane - 2, rows, :] for f in range(fields)]
            for f in range(fields):
                columns.append(advance(v2, 2, extra_of(terms, t, f), f, plane, y, weights))
            block = (plane - DEPTH) * blocks + t
            for g in range(len(columns) // 2):
                pair = jnp.concatenate(columns[2 * g : 2 * g + 2], 0)
                high = pair.astype(BF16)
                high_ref[block, 16 * g : 16 * g + 16, :] = high
                low_ref[block, 16 * g : 16 * g + 16, :] = (pair - high.astype(F32)).astype(BF16)

    def products(plane):
        base = (plane - DEPTH) * blocks
        high = jnp.concatenate([high_ref[base + t] for t in range(blocks)], 1)
        low = jnp.concatenate([low_ref[base + t] for t in range(blocks)], 1)
        both = jnp.concatenate([high, low], 0)
        acc[...] += lax.dot_general(
            both, high, (((1,), (1,)), ((), ())), preferred_element_type=F32
        )

    acc[...] = jnp.zeros_like(acc)

    @pl.loop(1, 4)
    def _(front):
        first_power(front, beyond(front, base1, ends))

    @pl.loop(4, 7)
    def _(front):
        terms = beyond(front, base2, ends)
        second_power(front - 2, terms[: base1 - base2])
        first_power(front, terms[base1 - base2 :])

    def whole_wave(front):
        terms = beyond(front, 0, ends)
        last_power(front - 4, terms[:base2])
        second_power(front - 2, terms[base2:base1])
        first_power(front, terms[base1:])

    whole_wave(7)

    whole_wave(8)
    products(3)

    @pl.loop(0, (nx - 4) // 2)
    def _(step):
        front = 9 + 2 * step
        whole_wave(front)
        products(front - 5)
        whole_wave(front + 1)
        products(front - 4)

    terms = beyond(nx + 5, 0, base1)
    last_power(nx + 1, terms[:base2])
    second_power(nx + 3, terms[base2:])
    products(nx)
    last_power(nx + 2, beyond(nx + 6, 0, base2))
    products(nx + 1)
    products(nx + 2)

    rows = acc.shape[1]
    sums = acc[...]
    same = lax.broadcasted_iota(jnp.int32, sums.shape, 0) % 8 == (
        lax.broadcasted_iota(jnp.int32, sums.shape, 1) % 8
    )
    sums = jnp.where(same, sums, 0.0).reshape(2 * rows // 8, 8, rows).sum(1)
    pick = lax.broadcasted_iota(jnp.int32, (rows, LANES), 0) // 8 == (
        lax.broadcasted_iota(jnp.int32, (rows, LANES), 1)
    )
    small = jnp.dot(sums, pick.astype(F32), precision=lax.Precision.HIGHEST)
    order = rows // 8
    square[...] = jnp.zeros_like(square)
    square[0:order, :] = small[order : 2 * order, :]
    cross = small[order : 2 * order, :]
    gram_ref[...] = small[0:order, :] + cross + square[...].T[0:order, :]


def factor_and_solve(
    cells, order, nx, ny, gram_a, gram_b, high_ref, low_ref, out_ref, factor_ref, w_wide, w_low, held, sem
):
    blocks = ny // 8
    rows = 8 * order

    row = lax.broadcasted_iota(jnp.int32, (order, LANES), 0)
    lane = lax.broadcasted_iota(jnp.int32, (order, LANES), 1)
    work = (gram_a[...] + gram_b[...]) / cells
    work = jnp.where(lane < order, work, jnp.where(lane == row + 64, 1.0, 0.0))
    for start in range(0, order, 8):
        columns = [
            jnp.broadcast_to(work[:, j : j + 1], (order, LANES)) for j in range(start, start + 8)
        ]
        for k in range(8):
            j = start + k
            factor = jnp.where(row > j, columns[k] / columns[k][j : j + 1, :], 0.0)
            work = work - factor * work[j : j + 1, :]
            for m in range(k + 1, 8):
                columns[m] = columns[m] - factor * columns[m][j : j + 1, :]
    pivots = jnp.sum(jnp.where(lane == row, work, 0.0), 1, keepdims=True)
    work = work / jnp.sqrt(pivots)
    factor_ref[...] = jnp.where(lane >= row, work, 0.0)[:, :order]
    inverse = pltpu.roll(work, 64, 1)
    inverse = jnp.where(lane <= row, inverse, 0.0)
    high = inverse.astype(BF16)
    low = (inverse - high.astype(F32)).astype(BF16)
    spread = (
        lax.broadcasted_iota(jnp.int32, (rows, order), 0) // 8
        == lax.broadcasted_iota(jnp.int32, (rows, order), 1)
    ).astype(BF16)
    across = (
        lax.broadcasted_iota(jnp.int32, (LANES, rows), 1) // 8
        == lax.broadcasted_iota(jnp.int32, (LANES, rows), 0)
    ).astype(BF16)
    same = lax.broadcasted_iota(jnp.int32, (rows, rows), 0) % 8 == (
        lax.broadcasted_iota(jnp.int32, (rows, rows), 1) % 8
    )

    def kron(small):
        tall = jnp.dot(spread, small, preferred_element_type=F32).astype(BF16)
        full = jnp.dot(tall, across, preferred_element_type=F32)
        return jnp.where(same, full, 0.0).astype(BF16)

    w_high = kron(high)
    w_wide[:, :rows] = w_high
    w_wide[:, rows:] = w_high
    w_low[...] = kron(low)

    def solve(plane):
        base = plane * blocks
        high = jnp.concatenate([high_ref[base + t] for t in range(blocks)], 1)
        low = jnp.concatenate([low_ref[base + t] for t in range(blocks)], 1)
        both = jnp.concatenate([high, low], 0)
        result = jnp.dot(w_wide[...], both, preferred_element_type=F32)
        result = result + jnp.dot(w_low[...], high, preferred_element_type=F32)
        for t in range(blocks):
            for b in range(order):
                held[b, plane, 8 * t : 8 * t + 8, :] = result[
                    8 * b : 8 * b + 8, LANES * t : LANES * t + LANES
                ]

    def store(step):
        part = pl.ds(step * TOGETHER, TOGETHER)
        return pltpu.make_async_copy(held.at[:, part], out_ref.at[:, part], sem.at[step])

    @pl.loop(0, nx // TOGETHER)
    def _(step):
        for u in range(TOGETHER):
            solve(step * TOGETHER + u)
        store(step).start()

    @pl.loop(0, nx // TOGETHER)
    def _(step):
        store(step).wait()


VM = functools.partial(pl.BlockSpec, memory_space=pltpu.VMEM)


def params(limit):
    return pltpu.CompilerParams(vmem_limit_bytes=limit * MIB)


def on_device(right_sides, permeability):
    fields, nx, ny, nz = right_sides.shape
    slabs = fields + 1
    order = fields * (DEPTH + 1)
    rows = 8 * order
    tall = ny + 16
    wide = nx + 2 * DEPTH
    strip_rows = ny + 8
    two_z = lax.axis_size("gz") > 2
    devices = lax.axis_size("gx") * lax.axis_size("gy") * lax.axis_size("gz")
    cells = float(nx * ny * nz * devices)

    pad_type = pltpu.VMEM((slabs, wide, tall, LANES), F32)
    x_type = pltpu.VMEM((slabs, DEPTH, ny, LANES), F32)
    y_type = pltpu.VMEM((slabs * nx * DEPTH, LANES), F32)
    e_rows = 8 * ((slabs * 2 * DEPTH * DEPTH + 7) // 8)
    e_type = pltpu.VMEM((e_rows, LANES), F32)
    pad, xa, xb, ya, yb = pl.pallas_call(
        pack_faces,
        out_shape=(pad_type, x_type, x_type, y_type, y_type),
        in_specs=[pl.BlockSpec(memory_space=pltpu.HBM)] * 2,
        out_specs=(VM(),) * 5,
        scratch_shapes=[pltpu.SemaphoreType.DMA((slabs,))],
        compiler_params=params(46),
        name="pack_faces",
    )(right_sides, permeability)
    got_ya, got_yb = pair_exchange(ya, yb, "gy")
    got_xa, got_xb = pair_exchange(xa, xb, "gx")
    inner = pl.pallas_call(
        functools.partial(inner_strips, nx, ny),
        out_shape=pltpu.VMEM((slabs, ny // 8, 2, 8, LANES), F32),
        in_specs=[VM()],
        out_specs=VM(),
        compiler_params=params(8),
        name="inner_strips",
        cost_estimate=pl.CostEstimate(flops=slabs * nx * ny * nz * 200, bytes_accessed=4 * slabs * nx * ny * nz, transcendentals=0),
    )(pad)
    ea, eb = pl.pallas_call(
        pack_edges,
        out_shape=(e_type, e_type),
        in_specs=[VM()] * 2,
        out_specs=(VM(),) * 2,
        compiler_params=params(8),
        name="pack_edges",
    )(got_xa, got_xb)
    got_ea, got_eb = pair_exchange(ea, eb, "gy")

    own_type = pltpu.VMEM((slabs, 2, strip_rows, LANES), F32)
    z_type = pltpu.VMEM((slabs, strip_rows, LANES), F32)
    z_count = 2 if two_z else 1
    outs = pl.pallas_call(
        functools.partial(assemble, nx, ny, two_z),
        out_shape=(pad_type, own_type) + (z_type,) * z_count,
        in_specs=[VM()] * 8,
        out_specs=(VM(),) * (2 + z_count),
        input_output_aliases={0: 0},
        compiler_params=params(8),
        name="assemble",
    )(pad, inner, got_xa, got_xb, got_ya, got_yb, got_ea, got_eb)
    pad, own = outs[:2]
    got_z = pair_exchange(outs[2], outs[-1], "gz")

    faces = pl.pallas_call(
        functools.partial(plane_faces, nx, ny),
        out_shape=pltpu.VMEM((6, nx + 4, tall, LANES), F32),
        in_specs=[VM()],
        out_specs=VM(),
        compiler_params=params(8),
        name="plane_faces",
        cost_estimate=pl.CostEstimate(
            flops=nx * ny * nz * 2000, bytes_accessed=28 * nx * ny * nz, transcendentals=0
        ),
    )(pad)

    blocks = nx * ny // 8
    split_type = pltpu.VMEM((blocks, rows, LANES), BF16)
    high, low, gram = pl.pallas_call(
        functools.partial(powers, nx, ny, two_z),
        out_shape=(split_type, split_type, pltpu.VMEM((order, LANES), F32)),
        in_specs=[VM()] * (3 + len(got_z)),
        out_specs=(VM(),) * 3,
        scratch_shapes=[
            pltpu.VMEM((6, nx + 4, tall, LANES), F32),
            pltpu.VMEM((fields, nx + 4, tall, LANES), F32),
            pltpu.VMEM((fields, nx + 2, tall, LANES), F32),
            pltpu.VMEM((slabs, 5, tall, LANES), F32),
            pltpu.VMEM((6, 3, tall, LANES), F32),
            pltpu.VMEM((fields, 3, tall, LANES), F32),
            pltpu.VMEM((fields, tall, LANES), F32),
            pltpu.VMEM((2 * rows, rows), F32),
            pltpu.VMEM((LANES, LANES), F32),
            pltpu.VMEM((fields * (ny + 2 * strip_rows), 2 * LANES), BF16),
        ],
        compiler_params=params(26),
        name="powers",
    )(pad, own, faces, *got_z)

    stages = []
    for axis in ("gz", "gx", "gy"):
        count, stride = lax.axis_size(axis), 1
        while stride < count:
            stages.append((axis, [(i, i ^ stride) for i in range(count)]))
            stride *= 2
    for axis, pairs in stages[:-1]:
        gram = gram + lax.ppermute(gram, axis, pairs)
    other = lax.ppermute(gram, *stages[-1])

    basis_q, factor_r = pl.pallas_call(
        functools.partial(factor_and_solve, cells, order, nx, ny),
        out_shape=(
            jax.ShapeDtypeStruct((order, nx, ny, nz), F32),
            jax.ShapeDtypeStruct((order, order), F32),
        ),
        in_specs=[VM()] * 4,
        out_specs=(pl.BlockSpec(memory_space=pltpu.HBM), VM()),
        scratch_shapes=[
            pltpu.VMEM((rows, 2 * rows), BF16),
            pltpu.VMEM((rows, rows), BF16),
            pltpu.VMEM((order, nx, ny, nz), F32),
            pltpu.SemaphoreType.DMA((nx // TOGETHER,)),
        ],
        compiler_params=params(24),
        name="factor_and_solve",
    )(gram, other, high, low)
    return (basis_q, factor_r)


def solution(mesh):
    placed = (P(None, "gx", "gy", "gz"), P("gx", "gy", "gz"))
    return jax.shard_map(
        on_device,
        mesh=mesh,
        in_specs=placed,
        out_specs=(P(None, "gx", "gy", "gz"), P()),
        check_vma=False,
    )
```

```python
import functools

import jax
import jax.numpy as jnp
from jax import lax
from jax.experimental import pallas as pl
from jax.experimental.pallas import tpu as pltpu
from jax.sharding import PartitionSpec as P

F32 = jnp.float32
BF16 = jnp.bfloat16
DEPTH = 3
LANES = 128
TOP = 8
MIB = 1 << 20
TOGETHER = 4


def even_on(axis):
    return lax.rem(lax.axis_index(axis), 2) == 0


def lane_index(rows=8):
    return lax.broadcasted_iota(jnp.int32, (rows, LANES), 1)


def take_lanes(tile, lanes):
    return jnp.take_along_axis(tile, lanes, axis=1)


def pair_exchange(first, second, axis):
    count = lax.axis_size(axis)
    firsts = [(i, i + 1) for i in range(0, count - 1, 2)]
    seconds = [(i, i + 1) for i in range(1, count - 1, 2)]
    got_first = lax.ppermute(first, axis, [p for a, b in firsts for p in ((a, b), (b, a))])
    if not seconds:
        return (got_first,)
    got_second = lax.ppermute(second, axis, [p for a, b in seconds for p in ((a, b), (b, a))])
    return (got_first, got_second)


def pack_faces(rs_ref, k_ref, pad_ref, xa_ref, xb_ref, ya_ref, yb_ref, sems):
    fields = rs_ref.shape[0]
    nx, ny = k_ref.shape[0], k_ref.shape[1]
    copies = [
        pltpu.make_async_copy(
            rs_ref.at[f], pad_ref.at[f, pl.ds(DEPTH, nx), pl.ds(TOP, ny)], sems.at[f]
        )
        for f in range(fields)
    ]
    copies.append(
        pltpu.make_async_copy(
            k_ref, pad_ref.at[fields, pl.ds(DEPTH, nx), pl.ds(TOP, ny)], sems.at[fields]
        )
    )
    for copy in copies:
        copy.start()
    ex, ey = even_on("gx"), even_on("gy")
    start_a = jnp.where(ex, nx, DEPTH)
    start_b = jnp.where(ex, DEPTH, nx)
    for f in range(fields + 1):
        copies[f].wait()
        for i in range(DEPTH):
            xa_ref[f, i] = pad_ref[f, start_a + i, TOP : TOP + ny, :]
            xb_ref[f, i] = pad_ref[f, start_b + i, TOP : TOP + ny, :]
        for x in range(nx):
            low = pad_ref[f, x + DEPTH, TOP : TOP + DEPTH, :]
            high = pad_ref[f, x + DEPTH, TOP + ny - DEPTH : TOP + ny, :]
            row = DEPTH * (f * nx + x)
            ya_ref[row : row + DEPTH, :] = jnp.where(ey, high, low)
            yb_ref[row : row + DEPTH, :] = jnp.where(ey, low, high)


CORNERS = ((1, 1), (1, 2), (2, 1))


def pack_edges(xa_ref, xb_ref, ea_ref, eb_ref):
    fields, _, ny, _ = xa_ref.shape
    ex, ey = even_on("gx"), even_on("gy")
    for f in range(fields):
        for side in range(2):
            a, b = (xa_ref, xb_ref) if side == 0 else (xb_ref, xa_ref)
            for c, (dx, dy) in enumerate(CORNERS):
                i = DEPTH - dx if side == 0 else dx - 1
                low = jnp.where(ex, b[f, i, dy - 1 : dy, :], a[f, i, dy - 1 : dy, :])
                high = jnp.where(ex, b[f, i, ny - dy : ny - dy + 1, :], a[f, i, ny - dy : ny - dy + 1, :])
                row = len(CORNERS) * (2 * f + side) + c
                ea_ref[row : row + 1, :] = jnp.where(ey, high, low)
                eb_ref[row : row + 1, :] = jnp.where(ey, low, high)


def assemble(nx, ny, two_z, pad_in, inner, xa, xb, ya, yb, ea, eb, *outs):
    del pad_in
    if two_z:
        pad, own, za, zb = outs
    else:
        pad, own, za = outs
        zb = None
    slabs = pad.shape[0]
    ex, ey, ez = even_on("gx"), even_on("gy"), even_on("gz")
    bottom = TOP + ny
    wide = nx + 2 * DEPTH
    half = wide // 2
    tiles = ny // 8 + 1
    for f in range(slabs):
        for i in range(DEPTH):
            a, b = xa[f, i], xb[f, i]
            pad[f, i, TOP:bottom, :] = jnp.where(ex, b, a)
            pad[f, nx + DEPTH + i, TOP:bottom, :] = jnp.where(ex, a, b)
        for x in range(nx):
            row = DEPTH * (f * nx + x)
            a, b = ya[row : row + DEPTH, :], yb[row : row + DEPTH, :]
            pad[f, x + DEPTH, TOP - DEPTH : TOP, :] = jnp.where(ey, b, a)
            pad[f, x + DEPTH, bottom : bottom + DEPTH, :] = jnp.where(ey, a, b)
        empty = jnp.zeros((DEPTH, LANES), F32)
        for side in range(2):
            for i in range(DEPTH):
                plane = i if side == 0 else nx + DEPTH + i
                pad[f, plane, TOP - DEPTH : TOP, :] = empty
                pad[f, plane, bottom : bottom + DEPTH, :] = empty
            for c, (dx, dy) in enumerate(CORNERS):
                plane = DEPTH - dx if side == 0 else nx + DEPTH - 1 + dx
                row = len(CORNERS) * (2 * f + side) + c
                a, b = ea[row : row + 1, :], eb[row : row + 1, :]
                pad[f, plane, TOP - dy : TOP - dy + 1, :] = jnp.where(ey, b, a)
                pad[f, plane, bottom + dy - 1 : bottom + dy, :] = jnp.where(ey, a, b)

    lane = lane_index()
    place = lane // 2
    is_left = lane % 2 == 1
    column = lane % wide
    step = jnp.minimum(lane // wide, DEPTH - 1)
    upper = lax.broadcasted_iota(jnp.int32, (8, LANES), 0) < 4

    def from_halves(first, second, at, zs):
        in_first = at < half
        index = 6 * jnp.where(in_first, at, jnp.minimum(at - half, half - 1)) + zs
        return jnp.where(in_first, take_lanes(first, index), take_lanes(second, index))

    @pl.loop(0, slabs)
    def _(f):
        for t in range(tiles):
            packed = []
            for part in range(2):
                if t < tiles - 1:
                    acc = inner[f, t, part]
                    todo = range(DEPTH) if part == 0 else range(half - DEPTH, half)
                else:
                    acc = jnp.zeros((8, LANES), F32)
                    todo = range(half)
                for m in todo:
                    plane = part * half + m
                    if t < tiles - 1:
                        tile = pad[f, plane, TOP + 8 * t : TOP + 8 * t + 8, :]
                    else:
                        tile = jnp.where(
                            upper,
                            pad[f, plane, TOP - DEPTH : TOP - DEPTH + 8, :],
                            pad[f, plane, bottom - 4 : bottom + 4, :],
                        )
                    acc = jnp.where(lane // 6 == m, pltpu.roll(tile, 6 * m + 3, 1), acc)
                packed.append(acc)
            first, second = packed
            out = slice(8 * t, 8 * t + 8)
            for j in range(2):
                own[f, j, out, :] = from_halves(
                    first, second, place, jnp.where(is_left, 3 + j, 2 - j)
                )
            to_left, to_right = 3 + step, 2 - step
            za[f, out, :] = from_halves(first, second, column, jnp.where(ez, to_right, to_left))
            if two_z:
                zb[f, out, :] = from_halves(
                    first, second, column, jnp.where(ez, to_left, to_right)
                )


def inner_strips(nx, ny, pad, inner):
    half = nx // 2 + DEPTH
    lane = lane_index()

    @pl.loop(0, pad.shape[0])
    def _(f):
        for t in range(ny // 8):
            for part in range(2):
                acc = jnp.zeros((8, LANES), F32)
                for m in range(DEPTH, half) if part == 0 else range(half - DEPTH):
                    tile = pad[f, part * half + m, TOP + 8 * t : TOP + 8 * t + 8, :]
                    acc = jnp.where(lane // 6 == m, pltpu.roll(tile, 6 * m + 3, 1), acc)
                inner[f, t, part] = acc


def face(center, other):
    total = center + other
    return 2.0 * center * other / jnp.where(total > 0, total, 1.0)


def plane_faces(nx, ny, pad, faces):
    fields = pad.shape[0] - 1
    lane = lane_index()

    @pl.loop(0, nx + 4, unroll=2)
    def _(i):
        plane = i + 1
        for t in range((ny + 2 * DEPTH + 7) // 8):
            r = TOP - 2 + 8 * t
            tile = pad[fields, plane, r : r + 8, :]
            beside = face(tile, pltpu.roll(tile, LANES - 1, 1))
            beside = jnp.where(lane == LANES - 1, 0.0, beside)
            found = [
                face(tile, pad[fields, plane + 1, r : r + 8, :]),
                face(tile, pad[fields, plane - 1, r : r + 8, :]),
                face(tile, pad[fields, plane, r + 1 : r + 9, :]),
                face(tile, pad[fields, plane, r - 1 : r + 7, :]),
                beside,
                pltpu.roll(beside, 1, 1),
            ]
            for n, weight in enumerate(found):
                faces[n, i, 8 * t : 8 * t + 8, :] = weight


def scaled_faces(center, others):
    faces = [face(center, other) for other in others]
    diagonal = faces[0]
    for weight in faces[1:]:
        diagonal = diagonal + weight
    scale = 2.5 / jnp.where(diagonal > 0, diagonal, 1.0)
    return [weight * scale for weight in faces]


def weighted(weights, values):
    accum = weights[0] * values[0]
    for weight, value in zip(weights[1:], values[1:]):
        accum = accum + weight * value
    return accum


def powers(nx, ny, two_z, pad, own, faces, za, *rest):
    if two_z:
        zb, rest = rest[0], rest[1:]
    else:
        zb = None
    high_ref, low_ref, gram_ref, coef, v1, v2, strip, scoef, s1, s2, acc, square, edge = rest
    fields = pad.shape[0] - 1
    wide = nx + 2 * DEPTH
    ez = even_on("gz")
    lane = lane_index()
    place = lane // 2
    is_left = lane % 2 == 1
    tiles = (ny + 2 * DEPTH + 7) // 8

    @pl.loop(0, fields + 1)
    def _(f):
        def put(q, t, tile):
            if t < ny // 8:
                strip[f, q, DEPTH + 8 * t : DEPTH + 8 * t + 8, :] = tile
            else:
                strip[f, q, 0:DEPTH, :] = tile[0:DEPTH, :]
                strip[f, q, DEPTH + ny : 2 * DEPTH + ny, :] = tile[4 : 4 + DEPTH, :]

        for t in range(ny // 8 + 1):
            rows = slice(8 * t, 8 * t + 8)
            got_a = za[f, rows, :]
            if two_z:
                got_b = zb[f, rows, :]
                left = jnp.where(ez, got_b, got_a)
                right = jnp.where(ez, got_a, got_b)
            for q in range(DEPTH):
                index = jnp.minimum(wide * (DEPTH - 1 - q) + place, LANES - 1)
                if two_z:
                    tile = jnp.where(is_left, take_lanes(left, index), take_lanes(right, index))
                else:
                    keep = is_left != ez
                    tile = jnp.where(keep, take_lanes(got_a, index), 0.0)
                put(q, t, tile)
            for j in range(2):
                put(DEPTH + j, t, own[f, j, rows, :])

    def strip_neighbours(ref, f, q, base, row):
        rows = slice(row, row + 8)
        tile = ref[f, q - base, rows, :]
        return tile, [
            pltpu.roll(tile, LANES - 2, 1),
            pltpu.roll(tile, 2, 1),
            ref[f, q - base, row + 1 : row + 9, :],
            ref[f, q - base, row - 1 : row + 7, :],
            ref[f, q + 1 - base, rows, :],
            ref[f, q - 1 - base, rows, :],
        ]

    for q in range(1, 4):
        for t in range(tiles):
            row = 1 + 8 * t
            center, others = strip_neighbours(strip, fields, q, 0, row)
            for n, weight in enumerate(scaled_faces(center, others)):
                scoef[n, q - 1, row : row + 8, :] = weight

    @pl.loop(0, fields)
    def _(f):
        for q in range(1, 4):
            for t in range(tiles):
                row = 1 + 8 * t
                weights = [scoef[n, q - 1, row : row + 8, :] for n in range(6)]
                _, values = strip_neighbours(strip, f, q, 0, row)
                s1[f, q - 1, row : row + 8, :] = weighted(weights, values)
        for t in range(tiles):
            row = 2 + 8 * t
            weights = [scoef[n, 1, row : row + 8, :] for n in range(6)]
            _, values = strip_neighbours(s1, f, 2, 1, row)
            s2[f, row : row + 8, :] = weighted(weights, values)

    def fill(base, count, y, lag, values_at):
        for t in range(count):
            row = y + DEPTH + 8 * t
            weight = scoef[5, 2, row : row + 8, :]
            for g in range(fields // 2):
                pair = [
                    pltpu.roll(weight * values_at(f, slice(row, row + 8)), 2 * lag, 1)
                    if lag
                    else weight * values_at(f, slice(row, row + 8))
                    for f in (2 * g, 2 * g + 1)
                ]
                pair = jnp.concatenate(pair, 0)
                high = pair.astype(BF16)
                at = base + 8 * (t * fields + 2 * g)
                edge[at : at + 16, :LANES] = high
                edge[at : at + 16, LANES:] = (pair - high.astype(F32)).astype(BF16)

    base2 = fields * ny
    base1 = base2 + 8 * fields * tiles
    ends = base1 + 8 * fields * tiles
    fill(0, ny // 8, 0, 4, lambda f, rows: s2[f, rows, :])
    fill(base2, tiles, -1, 2, lambda f, rows: s1[f, 1, rows, :])
    fill(base1, tiles, -2, 0, lambda f, rows: strip[f, 2, rows, :])

    def chosen(front):
        lanes = lane_index(LANES)
        source = jnp.where(
            lanes == 0, 2 * front + 1, jnp.where(lanes == LANES - 1, 2 * front, -1)
        )
        one_hot = lax.broadcasted_iota(jnp.int32, (LANES, LANES), 0) == source
        one_hot = jnp.where(one_hot, 1.0, 0.0).astype(BF16)
        return jnp.concatenate([one_hot, one_hot], 0)

    def beyond(front, start, stop):
        return jnp.dot(edge[start:stop, :], chosen(front), preferred_element_type=F32)

    @pl.loop(0, nx + 4, unroll=4)
    def _(i):
        plane = i + 1
        for t in range(tiles):
            y = 8 * t - 2
            tile = pad[fields, plane, TOP + y : TOP + y + 8, :]
            outside = pltpu.roll(strip[fields, 2, y + 3 : y + 11, :], LANES - 1 - 2 * plane, 1)
            weights = [faces[n, i, 8 * t : 8 * t + 8, :] for n in range(6)]
            diagonal = jnp.where(
                (lane == 0) | (lane == LANES - 1), face(tile, outside), 0.0
            )
            for weight in weights:
                diagonal = diagonal + weight
            scale = 2.5 / jnp.where(diagonal > 0, diagonal, 1.0)
            for n, weight in enumerate(weights):
                coef[n, i, 8 * t : 8 * t + 8, :] = weight * scale

    def advance(source, source_x, extra, f, plane, y, weights):
        r = TOP + y
        s = plane - source_x
        tile = source[f, s, r : r + 8, :]
        values = [
            source[f, s + 1, r : r + 8, :],
            source[f, s - 1, r : r + 8, :],
            source[f, s, r + 1 : r + 9, :],
            source[f, s, r - 1 : r + 7, :],
            pltpu.roll(tile, LANES - 1, 1),
            pltpu.roll(tile, 1, 1),
        ]
        return weighted(weights, values) + extra

    def weights_at(plane, y):
        return [coef[n, plane - 1, y + 2 : y + 10, :] for n in range(6)]

    def extra_of(terms, t, f):
        at = 8 * (t * fields + f)
        return terms[at : at + 8, :]

    def first_power(plane, terms):
        for t in range(tiles):
            y = 8 * t - 2
            weights = weights_at(plane, y)
            for f in range(fields):
                v1[f, plane - 1, TOP + y : TOP + y + 8, :] = advance(
                    pad, 0, extra_of(terms, t, f), f, plane, y, weights
                )

    def second_power(plane, terms):
        for t in range(tiles):
            y = 8 * t - 1
            weights = weights_at(plane, y)
            for f in range(fields):
                v2[f, plane - 2, TOP + y : TOP + y + 8, :] = advance(
                    v1, 1, extra_of(terms, t, f), f, plane, y, weights
                )

    blocks = ny // 8

    def last_power(plane, terms):
        for t in range(blocks):
            y = 8 * t
            rows = slice(TOP + y, TOP + y + 8)
            weights = weights_at(plane, y)
            columns = [pad[f, plane, rows, :] for f in range(fields)]
            columns += [v1[f, plane - 1, rows, :] for f in range(fields)]
            columns += [v2[f, plane - 2, rows, :] for f in range(fields)]
            for f in range(fields):
                columns.append(advance(v2, 2, extra_of(terms, t, f), f, plane, y, weights))
            block = (plane - DEPTH) * blocks + t
            for g in range(len(columns) // 2):
                pair = jnp.concatenate(columns[2 * g : 2 * g + 2], 0)
                high = pair.astype(BF16)
                high_ref[block, 16 * g : 16 * g + 16, :] = high
                low_ref[block, 16 * g : 16 * g + 16, :] = (pair - high.astype(F32)).astype(BF16)

    def products(plane):
        base = (plane - DEPTH) * blocks
        high = jnp.concatenate([high_ref[base + t] for t in range(blocks)], 1)
        low = jnp.concatenate([low_ref[base + t] for t in range(blocks)], 1)
        both = jnp.concatenate([high, low], 0)
        acc[...] += lax.dot_general(
            both, high, (((1,), (1,)), ((), ())), preferred_element_type=F32
        )

    acc[...] = jnp.zeros_like(acc)

    @pl.loop(1, 4)
    def _(front):
        first_power(front, beyond(front, base1, ends))

    @pl.loop(4, 7)
    def _(front):
        terms = beyond(front, base2, ends)
        second_power(front - 2, terms[: base1 - base2])
        first_power(front, terms[base1 - base2 :])

    def whole_wave(front):
        terms = beyond(front, 0, ends)
        last_power(front - 4, terms[:base2])
        second_power(front - 2, terms[base2:base1])
        first_power(front, terms[base1:])

    whole_wave(7)

    whole_wave(8)
    products(3)

    @pl.loop(0, (nx - 4) // 2)
    def _(step):
        front = 9 + 2 * step
        whole_wave(front)
        products(front - 5)
        whole_wave(front + 1)
        products(front - 4)

    terms = beyond(nx + 5, 0, base1)
    last_power(nx + 1, terms[:base2])
    second_power(nx + 3, terms[base2:])
    products(nx)
    last_power(nx + 2, beyond(nx + 6, 0, base2))
    products(nx + 1)
    products(nx + 2)

    rows = acc.shape[1]
    sums = acc[...]
    same = lax.broadcasted_iota(jnp.int32, sums.shape, 0) % 8 == (
        lax.broadcasted_iota(jnp.int32, sums.shape, 1) % 8
    )
    sums = jnp.where(same, sums, 0.0).reshape(2 * rows // 8, 8, rows).sum(1)
    pick = lax.broadcasted_iota(jnp.int32, (rows, LANES), 0) // 8 == (
        lax.broadcasted_iota(jnp.int32, (rows, LANES), 1)
    )
    small = jnp.dot(sums, pick.astype(F32), precision=lax.Precision.HIGHEST)
    order = rows // 8
    square[...] = jnp.zeros_like(square)
    square[0:order, :] = small[order : 2 * order, :]
    cross = small[order : 2 * order, :]
    gram_ref[...] = small[0:order, :] + cross + square[...].T[0:order, :]


def factor_and_solve(
    cells, order, nx, ny, gram_a, gram_b, high_ref, low_ref, out_ref, factor_ref, w_wide, w_low, held, sem
):
    blocks = ny // 8
    rows = 8 * order

    row = lax.broadcasted_iota(jnp.int32, (order, LANES), 0)
    lane = lax.broadcasted_iota(jnp.int32, (order, LANES), 1)
    work = (gram_a[...] + gram_b[...]) / cells
    work = jnp.where(lane < order, work, jnp.where(lane == row + 64, 1.0, 0.0))
    for start in range(0, order, 8):
        columns = [
            jnp.broadcast_to(work[:, j : j + 1], (order, LANES)) for j in range(start, start + 8)
        ]
        for k in range(8):
            j = start + k
            factor = jnp.where(row > j, columns[k] / columns[k][j : j + 1, :], 0.0)
            work = work - factor * work[j : j + 1, :]
            for m in range(k + 1, 8):
                columns[m] = columns[m] - factor * columns[m][j : j + 1, :]
    pivots = jnp.sum(jnp.where(lane == row, work, 0.0), 1, keepdims=True)
    work = work / jnp.sqrt(pivots)
    factor_ref[...] = jnp.where(lane >= row, work, 0.0)[:, :order]
    inverse = pltpu.roll(work, 64, 1)
    inverse = jnp.where(lane <= row, inverse, 0.0)
    high = inverse.astype(BF16)
    low = (inverse - high.astype(F32)).astype(BF16)
    spread = (
        lax.broadcasted_iota(jnp.int32, (rows, order), 0) // 8
        == lax.broadcasted_iota(jnp.int32, (rows, order), 1)
    ).astype(BF16)
    across = (
        lax.broadcasted_iota(jnp.int32, (LANES, rows), 1) // 8
        == lax.broadcasted_iota(jnp.int32, (LANES, rows), 0)
    ).astype(BF16)
    same = lax.broadcasted_iota(jnp.int32, (rows, rows), 0) % 8 == (
        lax.broadcasted_iota(jnp.int32, (rows, rows), 1) % 8
    )

    def kron(small):
        tall = jnp.dot(spread, small, preferred_element_type=F32).astype(BF16)
        full = jnp.dot(tall, across, preferred_element_type=F32)
        return jnp.where(same, full, 0.0).astype(BF16)

    w_high = kron(high)
    w_wide[:, :rows] = w_high
    w_wide[:, rows:] = w_high
    w_low[...] = kron(low)

    def solve(plane):
        base = plane * blocks
        high = jnp.concatenate([high_ref[base + t] for t in range(blocks)], 1)
        low = jnp.concatenate([low_ref[base + t] for t in range(blocks)], 1)
        both = jnp.concatenate([high, low], 0)
        result = jnp.dot(w_wide[...], both, preferred_element_type=F32)
        result = result + jnp.dot(w_low[...], high, preferred_element_type=F32)
        for t in range(blocks):
            for b in range(order):
                held[b, plane, 8 * t : 8 * t + 8, :] = result[
                    8 * b : 8 * b + 8, LANES * t : LANES * t + LANES
                ]

    def store(step):
        part = pl.ds(step * TOGETHER, TOGETHER)
        return pltpu.make_async_copy(held.at[:, part], out_ref.at[:, part], sem.at[step])

    @pl.loop(0, nx // TOGETHER)
    def _(step):
        for u in range(TOGETHER):
            solve(step * TOGETHER + u)
        store(step).start()

    @pl.loop(0, nx // TOGETHER)
    def _(step):
        store(step).wait()


VM = functools.partial(pl.BlockSpec, memory_space=pltpu.VMEM)


def params(limit):
    return pltpu.CompilerParams(vmem_limit_bytes=limit * MIB)


def on_device(right_sides, permeability):
    fields, nx, ny, nz = right_sides.shape
    slabs = fields + 1
    order = fields * (DEPTH + 1)
    rows = 8 * order
    tall = ny + 16
    wide = nx + 2 * DEPTH
    strip_rows = ny + 8
    two_z = lax.axis_size("gz") > 2
    devices = lax.axis_size("gx") * lax.axis_size("gy") * lax.axis_size("gz")
    cells = float(nx * ny * nz * devices)

    pad_type = pltpu.VMEM((slabs, wide, tall, LANES), F32)
    x_type = pltpu.VMEM((slabs, DEPTH, ny, LANES), F32)
    y_type = pltpu.VMEM((slabs * nx * DEPTH, LANES), F32)
    e_rows = 8 * ((slabs * 2 * len(CORNERS) + 7) // 8)
    e_type = pltpu.VMEM((e_rows, LANES), F32)
    pad, xa, xb, ya, yb = pl.pallas_call(
        pack_faces,
        out_shape=(pad_type, x_type, x_type, y_type, y_type),
        in_specs=[pl.BlockSpec(memory_space=pltpu.HBM)] * 2,
        out_specs=(VM(),) * 5,
        scratch_shapes=[pltpu.SemaphoreType.DMA((slabs,))],
        compiler_params=params(46),
        name="pack_faces",
    )(right_sides, permeability)
    got_ya, got_yb = pair_exchange(ya, yb, "gy")
    got_xa, got_xb = pair_exchange(xa, xb, "gx")
    inner = pl.pallas_call(
        functools.partial(inner_strips, nx, ny),
        out_shape=pltpu.VMEM((slabs, ny // 8, 2, 8, LANES), F32),
        in_specs=[VM()],
        out_specs=VM(),
        compiler_params=params(8),
        name="inner_strips",
        cost_estimate=pl.CostEstimate(flops=slabs * nx * ny * nz * 200, bytes_accessed=4 * slabs * nx * ny * nz, transcendentals=0),
    )(pad)
    ea, eb = pl.pallas_call(
        pack_edges,
        out_shape=(e_type, e_type),
        in_specs=[VM()] * 2,
        out_specs=(VM(),) * 2,
        compiler_params=params(8),
        name="pack_edges",
    )(got_xa, got_xb)
    got_ea, got_eb = pair_exchange(ea, eb, "gy")

    own_type = pltpu.VMEM((slabs, 2, strip_rows, LANES), F32)
    z_type = pltpu.VMEM((slabs, strip_rows, LANES), F32)
    z_count = 2 if two_z else 1
    outs = pl.pallas_call(
        functools.partial(assemble, nx, ny, two_z),
        out_shape=(pad_type, own_type) + (z_type,) * z_count,
        in_specs=[VM()] * 8,
        out_specs=(VM(),) * (2 + z_count),
        input_output_aliases={0: 0},
        compiler_params=params(8),
        name="assemble",
    )(pad, inner, got_xa, got_xb, got_ya, got_yb, got_ea, got_eb)
    pad, own = outs[:2]
    got_z = pair_exchange(outs[2], outs[-1], "gz")

    faces = pl.pallas_call(
        functools.partial(plane_faces, nx, ny),
        out_shape=pltpu.VMEM((6, nx + 4, tall, LANES), F32),
        in_specs=[VM()],
        out_specs=VM(),
        compiler_params=params(8),
        name="plane_faces",
        cost_estimate=pl.CostEstimate(
            flops=nx * ny * nz * 2000, bytes_accessed=28 * nx * ny * nz, transcendentals=0
        ),
    )(pad)

    blocks = nx * ny // 8
    split_type = pltpu.VMEM((blocks, rows, LANES), BF16)
    high, low, gram = pl.pallas_call(
        functools.partial(powers, nx, ny, two_z),
        out_shape=(split_type, split_type, pltpu.VMEM((order, LANES), F32)),
        in_specs=[VM()] * (3 + len(got_z)),
        out_specs=(VM(),) * 3,
        scratch_shapes=[
            pltpu.VMEM((6, nx + 4, tall, LANES), F32),
            pltpu.VMEM((fields, nx + 4, tall, LANES), F32),
            pltpu.VMEM((fields, nx + 2, tall, LANES), F32),
            pltpu.VMEM((slabs, 5, tall, LANES), F32),
            pltpu.VMEM((6, 3, tall, LANES), F32),
            pltpu.VMEM((fields, 3, tall, LANES), F32),
            pltpu.VMEM((fields, tall, LANES), F32),
            pltpu.VMEM((2 * rows, rows), F32),
            pltpu.VMEM((LANES, LANES), F32),
            pltpu.VMEM((fields * (ny + 2 * strip_rows), 2 * LANES), BF16),
        ],
        compiler_params=params(26),
        name="powers",
    )(pad, own, faces, *got_z)

    stages = []
    for axis in ("gz", "gx", "gy"):
        count, stride = lax.axis_size(axis), 1
        while stride < count:
            stages.append((axis, [(i, i ^ stride) for i in range(count)]))
            stride *= 2
    for axis, pairs in stages[:-1]:
        gram = gram + lax.ppermute(gram, axis, pairs)
    other = lax.ppermute(gram, *stages[-1])

    basis_q, factor_r = pl.pallas_call(
        functools.partial(factor_and_solve, cells, order, nx, ny),
        out_shape=(
            jax.ShapeDtypeStruct((order, nx, ny, nz), F32),
            jax.ShapeDtypeStruct((order, order), F32),
        ),
        in_specs=[VM()] * 4,
        out_specs=(pl.BlockSpec(memory_space=pltpu.HBM), VM()),
        scratch_shapes=[
            pltpu.VMEM((rows, 2 * rows), BF16),
            pltpu.VMEM((rows, rows), BF16),
            pltpu.VMEM((order, nx, ny, nz), F32),
            pltpu.SemaphoreType.DMA((nx // TOGETHER,)),
        ],
        compiler_params=params(24),
        name="factor_and_solve",
    )(gram, other, high, low)
    return (basis_q, factor_r)


def solution(mesh):
    placed = (P(None, "gx", "gy", "gz"), P("gx", "gy", "gz"))
    return jax.shard_map(
        on_device,
        mesh=mesh,
        in_specs=placed,
        out_specs=(P(None, "gx", "gy", "gz"), P()),
        check_vma=False,
    )
```
